512 devices in a mesh: box: 64 (over z_hi, y, x, core), samp: 8 (over z_lo).
Axes of the slice: x: 4, y: 4, z: 16 (z_hi: 2, z_lo: 8; z = z_hi * 8 + z_lo), core: 2. Of those that a mesh axis runs over, the one named last changes fastest.
Arguments:
- child_pattern: bfloat16 [2, 8, 512, 8192], P(None, 'samp', None, 'box'), may hold values from -6 to 6
- child_parent: int32 [8192], P('box'), may hold values from 0 to 2047, as said below
- child_octant: int32 [8192], P('box'), may hold values from 0 to 7, as said below
- child_sources: int32 [8192, 8], P('box'), may hold values from 0 to 8191, as said below
- child_offsets: int32 [8192, 8], P('box'), may hold values from 0 to 315
- child_counts: int32 [8192], P('box'), may hold values from 1 to 8, as said below
- parent_sources: int32 [2048, 8], replicated, may hold values from 0 to 2047
- parent_offsets: int32 [2048, 8], replicated, may hold values from 0 to 315
- parent_counts: int32 [2048], replicated, may hold values from 1 to 8, as said below
- interp_weights: bfloat16 [640, 2048], replicated, may hold values from -0.25 to 0.25
- shift_phase: float32 [8, 8, 2048], P(None, 'samp'), may hold values from -3.140625 to 3.140625
- child_table: bfloat16 [2, 316, 8, 512], P(None, None, 'samp'), may hold values from -4 to 4
- parent_table: bfloat16 [2, 316, 8, 2048], P(None, None, 'samp', 'box'), may hold values from -1.25 to 1.25
Outputs:
- child_field: bfloat16 [2, 8, 512, 8192], P(None, 'samp', None, 'box')
The draws below stay inside these ranges and needn't reach their ends.
Inputs may be any that keep to these rules, and one draw needn't show every extreme that they name: `child_parent`: child boxes on one index d of box have their parents among the boxes d * 32 to d * 32 + 31; children of one parent stand next to each other, parents in rising order; every parent has 2 to 8 children, and each index has parents with 8 and with 2. `child_octant`: children of one parent have different octants. `child_sources`: an entry of a child box's list names a child box of the same index of box, one of the last 32 boxes of the index before it, or one of the first 32 boxes of the index after it. Entries of child_sources and child_offsets at positions child_counts[c] and beyond are unused; on every index of box some child list is full. Entries of parent_sources and parent_offsets at positions parent_counts[p] and beyond are unused; some parent list is full.
All inputs are finite; a program needn't handle non-finite values.
Results may differ from the reference program's by a relative error of at most 0.0061.
Values may be sent and summed in bfloat16 or wider, within the bound.
A program may use at most 128 MiB of HBM per device.

```python
import jax
import jax.numpy as jnp
from jax import lax

CHILD_DEV = 128
PAR_DEV = 32
KCG = 512
KPG = 2048
RIM = 64
NOFF = 316
MC = 8
MP = 8
NEARB = 32
NG = 8
NBC = 8192
NBP = 2048


def octree_links(key):
    base = jax.random.fold_in(key, 7)
    first_key, second_key = jax.random.split(base)
    devices = NBC // CHILD_DEV
    orders = jax.vmap(lambda device_key: jax.random.permutation(device_key, PAR_DEV))(jax.random.split(first_key, devices))
    pattern = jnp.array([8, 2, 4, 2], dtype=jnp.int32)[jnp.arange(PAR_DEV) % 4]
    inverse = jnp.argsort(orders, axis=1)
    family = pattern[inverse]
    ends = jnp.cumsum(family, axis=1)
    slots = jnp.arange(CHILD_DEV, dtype=jnp.int32)
    local_parent = jnp.sum((ends[:, None, :] <= slots[None, :, None]).astype(jnp.int32), axis=2)
    starts = ends - family
    ranks = slots[None, :] - jnp.take_along_axis(starts, local_parent, axis=1)
    parents = local_parent + jnp.arange(devices, dtype=jnp.int32)[:, None] * PAR_DEV
    scores = jax.random.randint(second_key, (devices * PAR_DEV, 8), 0, 1 << 20) * 8 + jnp.arange(8, dtype=jnp.int32)[None, :]
    octants = jnp.argsort(scores, axis=1).astype(jnp.int32)
    child_octants = octants[parents.reshape(-1), ranks.reshape(-1)]
    return (parents.reshape(-1).astype(jnp.int32), child_octants.astype(jnp.int32))


def draw_child_parent(key, part):
    return octree_links(key)[0]


def draw_child_octant(key, part):
    return octree_links(key)[1]


def draw_child_sources(key, part):
    devices = NBC // CHILD_DEV
    keys = jax.random.split(jax.random.fold_in(key, 13), 3)
    region = jax.random.randint(keys[0], (NBC, MC), 0, 4)
    device_of = (jnp.arange(NBC, dtype=jnp.int32) // CHILD_DEV)[:, None]
    own_box = device_of * CHILD_DEV + jax.random.randint(keys[1], (NBC, MC), 0, CHILD_DEV)
    rim_pick = jax.random.randint(keys[2], (NBC, MC), 0, NEARB)
    left_box = (device_of - 1) * CHILD_DEV + CHILD_DEV - NEARB + rim_pick
    right_box = (device_of + 1) * CHILD_DEV + rim_pick
    use_left = (region == 2) & (device_of > 0)
    use_right = (region == 3) & (device_of < devices - 1)
    chosen = jnp.where(use_left, left_box, jnp.where(use_right, right_box, own_box)).astype(jnp.int32)
    chosen = chosen.at[0, 0].set(0)
    return chosen.at[NBC - 1, 0].set(NBC - 1)


def ragged_counts(key, total, longest, groups):
    keys = jax.random.split(key, 2)
    width_each = total // groups
    counts = jax.random.randint(keys[0], (groups, width_each), 1, longest + 1)
    spot = jax.random.randint(keys[1], (groups, 1), 0, width_each)
    filled = jnp.where(jnp.arange(width_each)[None, :] == spot, longest, counts)
    return filled.reshape(-1).astype(jnp.int32)


def draw_child_counts(key, part):
    return ragged_counts(jax.random.fold_in(key, 17), NBC, MC, NBC // CHILD_DEV)


def draw_parent_counts(key, part):
    return ragged_counts(jax.random.fold_in(key, 19), NBP, MP, 1)


def with_ends(values, own_key, low, high):
    extent = values.shape
    spot = [jax.random.randint(jax.random.fold_in(own_key, axis), (), 0, extent[axis]) for axis in range(len(extent))]
    values = values.at[tuple(spot)].set(low)
    longest = extent.index(max(extent))
    spot[longest] = (spot[longest] + 1) % extent[longest]
    return values.at[tuple(spot)].set(high)


def level_of(key, dims, pieces, low, top_value):
    gain = 1.0
    for position, shards_of in pieces:
        steps = jax.random.uniform(jax.random.fold_in(jax.random.fold_in(key, 6), position), (shards_of,), jnp.float32, low / len(pieces), top_value / len(pieces))
        gain = gain * jnp.repeat(jnp.exp(steps), dims[position] // shards_of).reshape((-1,) + (1,) * (len(dims) - 1 - position))
    return gain


def bell_draw(rng, shape, scale, bound, shards=(), kind=jnp.bfloat16):
    factor_of = level_of(rng, shape, shards, -0.22, 0.18) if shards else 1.0
    values = jax.random.normal(rng, shape, jnp.float32) * scale * factor_of
    return jnp.minimum(jnp.maximum(values, -bound), bound).astype(kind)


def setup_inputs(seed: int = 0) -> dict:
    seeds = jax.random.split(jax.random.key(seed), 14)
    return {
        "child_pattern": bell_draw(seeds[0], (2, NG, KCG, NBC), 1.0, 6.0, ((1, 8), (3, 64))),
        "child_parent": draw_child_parent(jax.random.fold_in(seeds[13], 71), 0),
        "child_octant": draw_child_octant(jax.random.fold_in(seeds[13], 71), 0),
        "child_sources": draw_child_sources(jax.random.fold_in(seeds[13], 71), 0),
        "child_offsets": with_ends(jax.random.randint(seeds[4], (NBC, MC), 0, NOFF), jax.random.fold_in(seeds[4], 1), 0, NOFF - 1).astype(jnp.int32),
        "child_counts": draw_child_counts(jax.random.fold_in(seeds[13], 71), 0),
        "parent_sources": with_ends(jax.random.randint(seeds[6], (NBP, MP), 0, NBP), jax.random.fold_in(seeds[6], 1), 0, NBP - 1).astype(jnp.int32),
        "parent_offsets": with_ends(jax.random.randint(seeds[7], (NBP, MP), 0, NOFF), jax.random.fold_in(seeds[7], 1), 0, NOFF - 1).astype(jnp.int32),
        "parent_counts": draw_parent_counts(jax.random.fold_in(seeds[13], 71), 0),
        "interp_weights": bell_draw(seeds[9], (KCG + 2 * RIM, KPG), (KCG + 2 * RIM) ** -0.5, 0.25),
        "shift_phase": jnp.clip(jax.random.uniform(seeds[10], (8, NG, KPG), jnp.float32, -3.140625, 3.140625), -3.140625, 3.140625),
        "child_table": bell_draw(seeds[11], (2, NOFF, NG, KCG), 0.25, 4.0, ((2, 8),)),
        "parent_table": bell_draw(seeds[12], (2, NOFF, NG, KPG), 0.08, 1.25, ((2, 8), (3, 64))),
    }


def complex_terms(coefficient, picked):
    return jnp.stack([coefficient[0] * picked[0] - coefficient[1] * picked[1], coefficient[0] * picked[1] + coefficient[1] * picked[0]])


def list_sum(pattern, table, sources, offsets, counts, slots):
    box_total = sources.shape[0]
    sample_count = pattern.shape[1]

    def advance(step_index, summed):
        picked = pattern[:, :, sources[:, step_index]].astype(jnp.float32)
        coefficient = jnp.transpose(table[:, offsets[:, step_index], :], (0, 2, 1)).astype(jnp.float32)
        alive = (step_index < counts)[None, None, :]
        return summed + jnp.where(alive, complex_terms(coefficient, picked), 0.0)

    return lax.fori_loop(0, slots, advance, jnp.zeros((2, sample_count, box_total), jnp.float32))


def reference(child_pattern, child_parent, child_octant, child_sources, child_offsets, child_counts, parent_sources, parent_offsets, parent_counts, interp_weights, shift_phase, child_table, parent_table):
    highest = lax.Precision.HIGHEST
    weights = interp_weights.astype(jnp.float32)
    flat_pattern = child_pattern.reshape(2, NG * KCG, NBC)
    groups = jnp.arange(NG, dtype=jnp.int32)

    def phases(group):
        angles = jnp.take(shift_phase, group, axis=1)
        return jnp.cos(angles)[child_octant].T, jnp.sin(angles)[child_octant].T

    def aggregate(group):
        positions = (group * KCG - RIM + jnp.arange(KCG + 2 * RIM, dtype=jnp.int32)) % (NG * KCG)
        extended = jnp.take(flat_pattern, positions.astype(jnp.int32), axis=1).astype(jnp.float32)
        interp = jnp.einsum("jk,rjc->rkc", weights, extended, precision=highest)
        cosine, sine_part = phases(group)
        shifted = jnp.stack([interp[0] * cosine - interp[1] * sine_part, interp[0] * sine_part + interp[1] * cosine])
        summed = jax.ops.segment_sum(jnp.transpose(shifted, (2, 0, 1)), child_parent, num_segments=NBP)
        return jnp.transpose(summed, (1, 2, 0)).astype(jnp.bfloat16)

    parent_pattern = lax.map(aggregate, groups)

    def parent_translate(group):
        table = jnp.take(parent_table, group, axis=2)
        return list_sum(parent_pattern[group], table, parent_sources, parent_offsets, parent_counts, MP).astype(jnp.bfloat16)

    parent_far = lax.map(parent_translate, groups)

    def disaggregate(group):
        field = parent_far[group][:, :, child_parent].astype(jnp.float32)
        cosine, sine_part = phases(group)
        lowered = jnp.stack([field[0] * cosine + field[1] * sine_part, field[1] * cosine - field[0] * sine_part]).astype(jnp.bfloat16)
        lowered = lax.optimization_barrier(lowered).astype(jnp.float32)
        return jnp.einsum("jk,rkc->rjc", weights, lowered, precision=highest).astype(jnp.bfloat16)

    child_terms = lax.map(disaggregate, groups)

    def finish(group):
        table = jnp.take(child_table, group, axis=2)
        pattern = jnp.take(child_pattern, group, axis=1)
        nearby = list_sum(pattern, table, child_sources, child_offsets, child_counts, MC)
        own_terms = child_terms[group].astype(jnp.float32)
        before = child_terms[(group - 1) % NG].astype(jnp.float32)
        after = child_terms[(group + 1) % NG].astype(jnp.float32)
        incoming = own_terms[:, RIM:RIM + KCG]
        incoming = incoming.at[:, :RIM].add(before[:, KCG + RIM:])
        incoming = incoming.at[:, KCG - RIM:].add(after[:, :RIM])
        return (nearby + incoming).astype(jnp.bfloat16)

    result = lax.map(finish, groups)
    return jnp.transpose(result, (1, 0, 2, 3))
```

```python
import functools

import jax
import jax.numpy as jnp
from jax import lax
from jax.experimental import pallas as pl
from jax.experimental.pallas import tpu as pltpu
from jax.sharding import PartitionSpec as P

PAR = 32
KCG = 512
KPG = 2048
RIM = 64
NOFF = 316
OFFPAD = 384
SLOTS = 256
F32 = jnp.float32
BF16 = jnp.bfloat16
NT = (((1,), (1,)), ((), ()))


def slot_matrix(slot_row):
    rows = lax.broadcasted_iota(jnp.int32, (SLOTS, 128), 0)
    return (rows == slot_row).astype(F32).astype(BF16)


def low_lanes(rows):
    return lax.broadcasted_iota(jnp.int32, (rows, 128), 1) < 64


def gather_up(own, left, right, w, cosine, sine, slot_row, send, ext, xs):
    ext[:, 0:RIM] = left[...]
    ext[:, RIM : RIM + KCG] = own[...]
    ext[:, RIM + KCG :] = right[...]
    sel = slot_matrix(slot_row[...])
    for r in range(2):
        xs[r * SLOTS : (r + 1) * SLOTS] = lax.dot_general(
            sel, ext[r], NT, preferred_element_type=F32
        ).astype(BF16)
    low = low_lanes(PAR)
    for t in range(4):
        parts = []
        for half in range(2):
            at = half * 1024 + 256 * t
            y = jnp.dot(xs[...], w[:, at : at + 256], preferred_element_type=F32)
            c = cosine[:, at : at + 256]
            s = sine[:, at : at + 256]
            re = im = None
            for o in range(8):
                yr = y[o * PAR : (o + 1) * PAR]
                yi = y[SLOTS + o * PAR : SLOTS + (o + 1) * PAR]
                co, so = c[o : o + 1], s[o : o + 1]
                tr = yr * co - yi * so
                ti = yr * so + yi * co
                re = tr if re is None else re + tr
                im = ti if im is None else im + ti
            parts.append((re, im))
        for u in range(2):
            for r in range(2):
                a = parts[0][r][:, 128 * u : 128 * u + 128]
                b = parts[1][r][:, 128 * u : 128 * u + 128]
                send[4 * t + 2 * u, r] = jnp.where(low, a, pltpu.roll(b, 64, 1)).astype(BF16)
                send[4 * t + 2 * u + 1, r] = jnp.where(low, pltpu.roll(a, 64, 1), b).astype(BF16)


def parent_rows(place, srow, toff, p0, p1, p2, p3, t0, t1, t2, t3, far, prow, tt, trow, acc):
    h, c = place[0], place[1]
    for j, ref in enumerate((p0, p1, p2, p3)):
        for q in range(16):
            for r in range(2):
                at = (j * 16 + q) * 64 + r * 32
                prow[at : at + 32] = ref[q, r].astype(F32)
    tt[...] = jnp.zeros_like(tt)
    for j, ref in enumerate((t0, t1, t2, t3)):
        hs = h + (j // 2) - 2 * h * (j // 2)
        cs = c + (j % 2) - 2 * c * (j % 2)
        at = pl.multiple_of(64 * hs + 32 * cs, 32)
        for r in range(2):
            tt[r, pl.ds(at, 32), 0:NOFF] = ref[r].astype(F32)
    for r in range(2):
        trow[r] = tt[r].T
    for q in range(16):
        column = (h * 32 + 2 * q + c) * 32

        def step(i, carry):
            for e in range(4):
                col = column + i * 4 + e
                re = im = None
                for m in range(8):
                    s = srow[m, col]
                    o = toff[m, col]
                    pr = prow[pl.ds(s, 1), :]
                    pi = prow[pl.ds(s + 32, 1), :]
                    tr = trow[0, pl.ds(o, 1), :]
                    ti = trow[1, pl.ds(o, 1), :]
                    x = tr * pr - ti * pi
                    y = tr * pi + ti * pr
                    re = x if re is None else re + x
                    im = y if im is None else im + y
                acc[0, pl.ds(i * 4 + e, 1), :] = re
                acc[1, pl.ds(i * 4 + e, 1), :] = im
            return carry

        lax.fori_loop(0, 8, step, 0)
        far[q] = acc[...].astype(BF16)


def spread_down(far, w, cosine, sine, slot_row, terms, lslot, lsel):
    sel = slot_matrix(slot_row[...])
    low = low_lanes(PAR)
    for t in range(8):
        tiles = []
        for r in range(2):
            a = far[2 * t, r].astype(F32)
            b = far[2 * t + 1, r].astype(F32)
            tiles.append((jnp.where(low, a, pltpu.roll(b, 64, 1)), jnp.where(low, pltpu.roll(a, 64, 1), b)))
        for half in range(2):
            fr, fi = tiles[0][half], tiles[1][half]
            at = half * 1024 + 128 * t
            for o in range(8):
                co = cosine[o : o + 1, at : at + 128]
                so = sine[o : o + 1, at : at + 128]
                lslot[0, o * PAR : (o + 1) * PAR, at : at + 128] = (fr * co + fi * so).astype(BF16)
                lslot[1, o * PAR : (o + 1) * PAR, at : at + 128] = (fi * co - fr * so).astype(BF16)
    for r in range(2):
        lsel[r * 128 : (r + 1) * 128] = lax.dot_general(
            sel, lslot[r], (((0,), (0,)), ((), ())), preferred_element_type=F32
        ).astype(BF16)
    out = lax.dot_general(w[...], lsel[...], NT, preferred_element_type=F32)
    for r in range(2):
        terms[r] = out[:, r * 128 : (r + 1) * 128].astype(BF16)


def near_lists(own, before, after, table, pos, off, near, ohs, oht):
    post = pos[...].T
    offt = off[...].T
    for m in range(8):
        srow = lax.broadcasted_iota(jnp.int32, (128, 256), 1).astype(F32)
        trow = lax.broadcasted_iota(jnp.int32, (128, OFFPAD), 1).astype(F32)
        ohs[m * 128 : (m + 1) * 128] = (post[:, m : m + 1] == srow).astype(F32).astype(BF16)
        oht[m * 128 : (m + 1) * 128] = (offt[:, m : m + 1] == trow).astype(F32).astype(BF16)
    for n in range(2):
        at = 256 * n
        ts, ps = [], []
        for r in range(2):
            ts.append(jnp.dot(oht[...], table[:, r * 512 + at : r * 512 + at + 256], preferred_element_type=F32))
            halo = jnp.concatenate([before[r, :, at : at + 256], after[r, :, at : at + 256]], axis=0)
            p = lax.dot_general(ohs[:, 0:128], own[r, at : at + 256], NT, preferred_element_type=F32)
            ps.append(p + jnp.dot(ohs[:, 128:192], halo, preferred_element_type=F32))
        re = ts[0] * ps[0] - ts[1] * ps[1]
        im = ts[0] * ps[1] + ts[1] * ps[0]
        for r, v in enumerate((re, im)):
            total = v[0:128]
            for m in range(1, 8):
                total = total + v[m * 128 : (m + 1) * 128]
            near[r, at : at + 256] = total.T


def finish(near, terms, low_rim, high_rim, out):
    for r in range(2):
        mid = terms[r, RIM : RIM + KCG].astype(F32)
        out[r, 0:RIM] = (near[r, 0:RIM] + (mid[0:RIM] + low_rim[r].astype(F32))).astype(BF16)
        out[r, RIM : KCG - RIM] = (near[r, RIM : KCG - RIM] + mid[RIM : KCG - RIM]).astype(BF16)
        out[r, KCG - RIM :] = (near[r, KCG - RIM :] + (mid[KCG - RIM :] + high_rim[r].astype(F32))).astype(BF16)


def call(body, out_shape, scratch, smem=0):
    def run(*args):
        vm = pl.BlockSpec(memory_space=pltpu.VMEM)
        sm = pl.BlockSpec(memory_space=pltpu.SMEM)
        return pl.pallas_call(
            body,
            out_shape=out_shape,
            in_specs=[sm] * smem + [vm] * (len(args) - smem),
            out_specs=vm,
            scratch_shapes=scratch,
            compiler_params=pltpu.CompilerParams(vmem_limit_bytes=60000 * 1024),
        )(*args)

    return run


def local(
    child_pattern,
    child_parent,
    child_octant,
    child_sources,
    child_offsets,
    child_counts,
    parent_sources,
    parent_offsets,
    parent_counts,
    interp_weights,
    shift_phase,
    child_table,
    parent_table,
):
    me = lax.axis_index("box")
    h, q, c = me // 32, (me // 2) % 16, me % 2
    boxes = range(64)
    own = child_pattern[:, 0]
    angles = shift_phase[:, 0, :]
    cosine, sine = jnp.cos(angles), jnp.sin(angles)
    slot_row = (child_octant * PAR + child_parent - me * PAR)[None, :]

    ring = [(i, (i + 1) % 8) for i in range(8)]
    back = [(j, i) for i, j in ring]
    left = lax.ppermute(own[:, KCG - RIM :], "samp", ring)
    right = lax.ppermute(own[:, :RIM], "samp", back)
    up = [(i, i + 1) for i in range(63)]
    down = [(i + 1, i) for i in range(63)]
    before = lax.ppermute(jnp.transpose(own[:, :, 96:], (0, 2, 1)), "box", up)
    after = lax.ppermute(jnp.transpose(own[:, :, :32], (0, 2, 1)), "box", down)
    other_core = [(i, i ^ 1) for i in boxes]
    other_half = [(i, i ^ 32) for i in boxes]
    plane = [[hh * 32 + 2 * qq + cc for qq in range(16)] for hh in range(2) for cc in range(2)]

    t0 = jnp.transpose(parent_table[:, :, 0, :], (0, 2, 1))
    t1 = lax.ppermute(t0, "box", other_core)
    t2 = lax.ppermute(t0, "box", other_half)
    t3 = lax.ppermute(t2, "box", other_core)

    send = call(
        gather_up,
        jax.ShapeDtypeStruct((16, 2, PAR, 128), BF16),
        [pltpu.VMEM((2, KCG + 2 * RIM, 128), BF16), pltpu.VMEM((2 * SLOTS, KCG + 2 * RIM), BF16)],
    )(own, left, right, interp_weights, cosine, sine, slot_row)

    p0 = lax.all_to_all(send, "box", 0, 0, axis_index_groups=plane, tiled=True)
    p2 = lax.ppermute(p0, "box", other_half)
    p1 = lax.ppermute(p0, "box", other_core)
    p3 = lax.ppermute(p2, "box", other_core)

    src = parent_sources.T
    dev = src // PAR
    hs, qs, cs = dev // 32, (dev // 2) % 16, dev % 2
    slot = (hs ^ h) * 2 + (cs ^ c)
    srow = (slot * 16 + qs) * 64 + src % PAR
    srow = jnp.clip(srow, 0, 4063)
    live = jnp.arange(8, dtype=jnp.int32)[:, None] < parent_counts[None, :]
    toff = jnp.where(live, parent_offsets.T, NOFF)
    place = jnp.stack([h, c]).astype(jnp.int32)
    far = call(
        parent_rows,
        jax.ShapeDtypeStruct((16, 2, PAR, 128), BF16),
        [
            pltpu.VMEM((4096, 128), F32),
            pltpu.VMEM((2, 128, OFFPAD), F32),
            pltpu.VMEM((2, OFFPAD, 128), F32),
            pltpu.VMEM((2, PAR, 128), F32),
        ],
        smem=3,
    )(place, srow, toff, p0, p1, p2, p3, t0, t1, t2, t3)
    back_far = lax.all_to_all(far, "box", 0, 0, axis_index_groups=plane, tiled=True)

    terms = call(
        spread_down,
        jax.ShapeDtypeStruct((2, KCG + 2 * RIM, 128), BF16),
        [pltpu.VMEM((2, SLOTS, KPG), BF16), pltpu.VMEM((256, KPG), BF16)],
    )(back_far, interp_weights, cosine, sine, slot_row)
    low_rim = lax.ppermute(terms[:, RIM + KCG :], "samp", ring)
    high_rim = lax.ppermute(terms[:, :RIM], "samp", back)

    rel = child_sources.T - me * 128
    pos = jnp.where(rel < 0, rel + 160, jnp.where(rel < 128, rel, rel + 32)).astype(F32)
    alive = jnp.arange(8, dtype=jnp.int32)[:, None] < child_counts[None, :]
    off = jnp.where(alive, child_offsets.T, OFFPAD).astype(F32)
    ctab = jnp.transpose(child_table[:, :, 0, :], (1, 0, 2)).reshape(NOFF, 1024)
    ctab = jnp.pad(ctab, ((0, OFFPAD - NOFF), (0, 0)))
    near = call(
        near_lists,
        jax.ShapeDtypeStruct((2, KCG, 128), F32),
        [pltpu.VMEM((1024, 256), BF16), pltpu.VMEM((1024, OFFPAD), BF16)],
    )(own, before, after, ctab, pos, off)
    out = call(finish, jax.ShapeDtypeStruct((2, KCG, 128), BF16), [])(near, terms, low_rim, high_rim)
    return out[:, None]


def solution(mesh):
    return jax.shard_map(
        local,
        mesh=mesh,
        in_specs=(
            P(None, "samp", None, "box"),
            P("box"),
            P("box"),
            P("box", None),
            P("box", None),
            P("box"),
            P(),
            P(),
            P(),
            P(),
            P(None, "samp", None),
            P(None, None, "samp", None),
            P(None, None, "samp", "box"),
        ),
        out_specs=P(None, "samp", None, "box"),
        check_vma=False,
    )
```

```python
import functools

import jax
import jax.numpy as jnp
from jax import lax
from jax.experimental import pallas as pl
from jax.experimental.pallas import tpu as pltpu
from jax.sharding import PartitionSpec as P

PAR = 32
KCG = 512
KPG = 2048
RIM = 64
NOFF = 316
OFFPAD = 384
SLOTS = 256
F32 = jnp.float32
BF16 = jnp.bfloat16
NT = (((1,), (1,)), ((), ()))


def slot_matrix(slot_row):
    rows = lax.broadcasted_iota(jnp.int32, (SLOTS, 128), 0)
    return (rows == slot_row).astype(F32).astype(BF16)


def low_lanes(rows):
    return lax.broadcasted_iota(jnp.int32, (rows, 128), 1) < 64


def copy_to(src, dst, send_sem, recv_sem, **device):
    return pltpu.make_async_remote_copy(
        src_ref=src,
        dst_ref=dst,
        send_sem=send_sem,
        recv_sem=recv_sem,
        device_id=device,
        device_id_type=pl.DeviceIdType.MESH,
    )


def near_lists(own, before, after, table, pos, off, near, ohs, oht):
    post = pos[...].T
    offt = off[...].T
    srow = lax.broadcasted_iota(jnp.int32, (128, 256), 1).astype(F32)
    trow = lax.broadcasted_iota(jnp.int32, (128, OFFPAD), 1).astype(F32)
    for m in range(8):
        ohs[m * 128 : (m + 1) * 128] = (post[:, m : m + 1] == srow).astype(F32).astype(BF16)
        oht[m * 128 : (m + 1) * 128] = (offt[:, m : m + 1] == trow).astype(F32).astype(BF16)
    for n in range(2):
        at = 256 * n
        ts, ps = [], []
        for r in range(2):
            ts.append(jnp.dot(oht[...], table[:, r * 512 + at : r * 512 + at + 256], preferred_element_type=F32))
            halo = jnp.concatenate([before[r, :, at : at + 256], after[r, :, at : at + 256]], axis=0)
            p = lax.dot_general(ohs[:, 0:128], own[r, at : at + 256], NT, preferred_element_type=F32)
            ps.append(p + jnp.dot(ohs[:, 128:192], halo, preferred_element_type=F32))
        re = ts[0] * ps[0] - ts[1] * ps[1]
        im = ts[0] * ps[1] + ts[1] * ps[0]
        for r, v in enumerate((re, im)):
            total = v[0:128]
            for m in range(1, 8):
                total = total + v[m * 128 : (m + 1) * 128]
            near[r, at : at + 256] = total.T


def whole(
    srow, toff, own, w, cosine, sine, slot_row, tpar, ctab, pos, off,
    out,
    halo_l, halo_r, box_b, box_a, bsend, tsend, tparts, xown, xrim, ybuf, send, prec,
    p4, tt, t4, acc, fsend, frecv, lslot, lsel, rsend, rim_lo, rim_hi, near, ohs, oht,
    halo_s, halo_d, box_s, box_d, t_s, t_d, pl_s, pl_d, cr_s, cr_d, co_s, co_d, re_s, re_d, rim_s, rim_d,
):
    d = lax.axis_index("box")
    g = lax.axis_index("samp")
    h, q, c = d // 32, (d // 2) % 16, d % 2
    gup, gdown = (g + 1) % 8, (g + 7) % 8
    mate = d + 1 - 2 * c
    far_half = (1 - h) * 32

    barrier = pltpu.get_barrier_semaphore()

    def greet(**device):
        pl.semaphore_signal(barrier, inc=1, device_id=device, device_id_type=pl.DeviceIdType.MESH)

    greet(samp=gup)
    greet(samp=gdown)
    for k in range(16):
        greet(box=far_half + 2 * k + c)
    for k in range(16):

        @pl.when(q != k)
        def _():
            greet(box=h * 32 + 2 * k + c)

    greet(box=mate)

    @pl.when(d < 63)
    def _():
        greet(box=d + 1)

    @pl.when(d > 0)
    def _():
        greet(box=d - 1)

    pick = lax.broadcasted_iota(jnp.int32, (PAR, 128), 0)
    lane = lax.broadcasted_iota(jnp.int32, (PAR, 128), 1)
    last = (pick + 96 == lane).astype(F32).astype(BF16)
    first = (pick == lane).astype(F32).astype(BF16)
    for r in range(2):
        bsend[0, r] = lax.dot_general(last, own[r], NT, preferred_element_type=F32).astype(BF16)
        bsend[1, r] = lax.dot_general(first, own[r], NT, preferred_element_type=F32).astype(BF16)
    tsend[...] = jnp.zeros_like(tsend)
    tsend[:, :, 0:NOFF] = tpar[...]

    @pl.when(d == 0)
    def _():
        box_b[...] = jnp.zeros_like(box_b)

    @pl.when(d == 63)
    def _():
        box_a[...] = jnp.zeros_like(box_a)

    sel = slot_matrix(slot_row[...])
    for r in range(2):
        xown[r * SLOTS : (r + 1) * SLOTS] = lax.dot_general(
            sel, own[r], NT, preferred_element_type=F32
        ).astype(BF16)
    for t in range(8):
        ybuf[:, 256 * t : 256 * t + 256] = jnp.dot(
            xown[...], w[RIM : RIM + KCG, 256 * t : 256 * t + 256], preferred_element_type=F32
        )

    pl.semaphore_wait(barrier, 34 + (d < 63).astype(jnp.int32) + (d > 0).astype(jnp.int32))

    to_up = copy_to(own.at[:, KCG - RIM :], halo_l, halo_s.at[0], halo_d.at[0], samp=gup)
    to_down = copy_to(own.at[:, :RIM], halo_r, halo_s.at[1], halo_d.at[1], samp=gdown)
    to_up.start()
    to_down.start()
    t_far = copy_to(tsend, tparts.at[1], t_s.at[0], t_d.at[0], box=far_half + 2 * q + c)
    t_mate = copy_to(tsend, tparts.at[0], t_s.at[1], t_d.at[1], box=mate)
    box_up = copy_to(bsend.at[0], box_b, box_s.at[0], box_d.at[0], box=d + 1)
    box_down = copy_to(bsend.at[1], box_a, box_s.at[1], box_d.at[1], box=d - 1)

    @pl.when(d < 63)
    def _():
        box_up.start()

    @pl.when(d > 0)
    def _():
        box_down.start()

    t_far.start()
    t_mate.start()

    to_up.wait_recv()
    to_down.wait_recv()
    for r in range(2):
        rows = pl.ds(r * SLOTS, SLOTS)
        xrim[rows, 0:RIM] = lax.dot_general(sel, halo_l[r], NT, preferred_element_type=F32).astype(BF16)
        xrim[rows, RIM : 2 * RIM] = lax.dot_general(sel, halo_r[r], NT, preferred_element_type=F32).astype(BF16)
    low = low_lanes(PAR)

    def plane_copy(k):
        return copy_to(send.at[k], prec.at[0, q], pl_s.at[k], pl_d.at[q], box=h * 32 + 2 * k + c)

    def cross_copy(k):
        return copy_to(send.at[k], prec.at[2, q], cr_s.at[k], cr_d.at[q], box=far_half + 2 * k + c)

    for t in range(4):
        parts = []
        for half in range(2):
            at = half * 1024 + 256 * t
            rim_w = jnp.concatenate([w[0:RIM, at : at + 256], w[RIM + KCG :, at : at + 256]], axis=0)
            y = ybuf[:, at : at + 256] + jnp.dot(xrim[...], rim_w, preferred_element_type=F32)
            cc = cosine[:, at : at + 256]
            ss = sine[:, at : at + 256]
            re = im = None
            for o in range(8):
                yr = y[o * PAR : (o + 1) * PAR]
                yi = y[SLOTS + o * PAR : SLOTS + (o + 1) * PAR]
                co, so = cc[o : o + 1], ss[o : o + 1]
                tr = yr * co - yi * so
                ti = yr * so + yi * co
                re = tr if re is None else re + tr
                im = ti if im is None else im + ti
            parts.append((re, im))
        for u in range(2):
            for r in range(2):
                a = parts[0][r][:, 128 * u : 128 * u + 128]
                b = parts[1][r][:, 128 * u : 128 * u + 128]
                send[4 * t + 2 * u, r] = jnp.where(low, a, pltpu.roll(b, 64, 1)).astype(BF16)
                send[4 * t + 2 * u + 1, r] = jnp.where(low, pltpu.roll(a, 64, 1), b).astype(BF16)
        for k in range(4 * t, 4 * t + 4):
            cross_copy(k).start()

            @pl.when(q != k)
            def _():
                plane_copy(k).start()

    prec[0, q] = send[q]

    def from_plane(k):
        return copy_to(send.at[k], prec.at[0, k], pl_s.at[k], pl_d.at[k], box=mate)

    def from_cross(k):
        return copy_to(send.at[k], prec.at[2, k], cr_s.at[k], cr_d.at[k], box=mate)

    def mate_copy(j, e):
        return copy_to(
            prec.at[j, pl.ds(4 * e, 4)], prec.at[j + 1, pl.ds(4 * e, 4)],
            co_s.at[2 * j + e], co_d.at[2 * j + e], box=mate,
        )

    def unpack(j, k):
        for r in range(2):
            v = prec[j, k, r].astype(F32)
            base = (j * 16 + k) * 128 + r
            p4[pl.ds(base, PAR, stride=4), :] = v
            p4[pl.ds(base + 2, PAR, stride=4), :] = v

    for e in range(4):
        for k in range(4 * e, 4 * e + 4):

            @pl.when(q != k)
            def _():
                from_plane(k).wait_recv()

        mate_copy(0, e).start()

    @pl.when(d > 0)
    def _():
        copy_to(bsend.at[0], box_b, box_s.at[0], box_d.at[0], box=mate).wait_recv()

    @pl.when(d < 63)
    def _():
        copy_to(bsend.at[1], box_a, box_s.at[1], box_d.at[1], box=mate).wait_recv()

    near_lists(own, box_b, box_a, ctab, pos, off, near, ohs, oht)

    t_far.wait_recv()
    t_second = copy_to(tparts.at[1], tparts.at[2], t_s.at[2], t_d.at[2], box=mate)
    t_second.start()
    t_mate.wait_recv()
    t_second.wait_recv()
    for j in range(4):
        hs = h + (j // 2) - 2 * h * (j // 2)
        cs = c + (j % 2) - 2 * c * (j % 2)
        at = pl.multiple_of(64 * hs + 32 * cs, 32)
        for r in range(2):
            tt[r, pl.ds(at, 32), :] = (tsend[r] if j == 0 else tparts[j - 1, r]).astype(F32)
    for r in range(2):
        turned = tt[r].T
        t4[pl.ds(2 * r, OFFPAD, stride=4), :] = turned
        t4[pl.ds(2 * r + 1, OFFPAD, stride=4), :] = turned

    for k in range(16):
        unpack(0, k)
    for e in range(4):
        mate_copy(0, e).wait_recv()
        for k in range(4 * e, 4 * e + 4):
            unpack(1, k)
    for e in range(4):
        for k in range(4 * e, 4 * e + 4):
            from_cross(k).wait_recv()
        mate_copy(2, e).start()
        for k in range(4 * e, 4 * e + 4):
            unpack(2, k)
    for e in range(4):
        mate_copy(2, e).wait_recv()
        for k in range(4 * e, 4 * e + 4):
            unpack(3, k)

    def target_block(k, carry):
        column = (h * 32 + 2 * k + c) * 32

        def step(i, inner):
            for e in range(8):
                col = column + i * 8 + e
                total = None
                for m in range(8):
                    s = srow[m, col]
                    o = toff[m, col]
                    v = p4[pl.ds(s, 4), :] * t4[pl.ds(o, 4), :]
                    total = v if total is None else total + v
                acc[pl.ds(pl.multiple_of(i * 32, 32) + 4 * e, 4), :] = total
            return inner

        lax.fori_loop(0, 4, step, 0)
        re = acc[pl.ds(0, PAR, stride=4), :] - acc[pl.ds(3, PAR, stride=4), :]
        im = acc[pl.ds(1, PAR, stride=4), :] + acc[pl.ds(2, PAR, stride=4), :]
        fsend[k, 0] = re.astype(BF16)
        fsend[k, 1] = im.astype(BF16)

        @pl.when(q != k)
        def _():
            copy_to(fsend.at[k], frecv.at[q], re_s.at[k], re_d.at[q], box=h * 32 + 2 * k + c).start()

        return carry

    lax.fori_loop(0, 16, target_block, 0)
    frecv[q] = fsend[q]

    for t in range(8):
        for k in range(2 * t, 2 * t + 2):

            @pl.when(q != k)
            def _():
                copy_to(fsend.at[k], frecv.at[k], re_s.at[k], re_d.at[k], box=mate).wait_recv()

        tiles = []
        for r in range(2):
            a = frecv[2 * t, r].astype(F32)
            b = frecv[2 * t + 1, r].astype(F32)
            tiles.append((jnp.where(low, a, pltpu.roll(b, 64, 1)), jnp.where(low, pltpu.roll(a, 64, 1), b)))
        for half in range(2):
            fr, fi = tiles[0][half], tiles[1][half]
            at = half * 1024 + 128 * t
            for o in range(8):
                co = cosine[o : o + 1, at : at + 128]
                so = sine[o : o + 1, at : at + 128]
                lslot[0, o * PAR : (o + 1) * PAR, at : at + 128] = (fr * co + fi * so).astype(BF16)
                lslot[1, o * PAR : (o + 1) * PAR, at : at + 128] = (fi * co - fr * so).astype(BF16)
    for r in range(2):
        lsel[r * 128 : (r + 1) * 128] = lax.dot_general(
            sel, lslot[r], (((0,), (0,)), ((), ())), preferred_element_type=F32
        ).astype(BF16)

    lows = lax.dot_general(w[0:RIM], lsel[...], NT, preferred_element_type=F32)
    highs = lax.dot_general(w[RIM + KCG :], lsel[...], NT, preferred_element_type=F32)
    for r in range(2):
        rsend[0, r] = lows[:, r * 128 : (r + 1) * 128].astype(BF16)
        rsend[1, r] = highs[:, r * 128 : (r + 1) * 128].astype(BF16)
    rim_down = copy_to(rsend.at[0], rim_hi, rim_s.at[0], rim_d.at[0], samp=gdown)
    rim_up = copy_to(rsend.at[1], rim_lo, rim_s.at[1], rim_d.at[1], samp=gup)
    rim_down.start()
    rim_up.start()
    mids = lax.dot_general(w[RIM : RIM + KCG], lsel[...], NT, preferred_element_type=F32)
    for r in range(2):
        mid = mids[:, r * 128 : (r + 1) * 128].astype(BF16).astype(F32)
        out[r, RIM : KCG - RIM] = (near[r, RIM : KCG - RIM] + mid[RIM : KCG - RIM]).astype(BF16)
        near[r, 0:RIM] = near[r, 0:RIM] + mid[0:RIM]
        near[r, KCG - RIM :] = near[r, KCG - RIM :] + mid[KCG - RIM :]
    rim_down.wait_recv()
    rim_up.wait_recv()
    for r in range(2):
        out[r, 0:RIM] = (near[r, 0:RIM] + rim_lo[r].astype(F32)).astype(BF16)
        out[r, KCG - RIM :] = (near[r, KCG - RIM :] + rim_hi[r].astype(F32)).astype(BF16)

    to_up.wait_send()
    to_down.wait_send()
    t_far.wait_send()
    t_mate.wait_send()
    t_second.wait_send()

    @pl.when(d < 63)
    def _():
        box_up.wait_send()

    @pl.when(d > 0)
    def _():
        box_down.wait_send()

    for k in range(16):
        cross_copy(k).wait_send()

        @pl.when(q != k)
        def _():
            plane_copy(k).wait_send()
            copy_to(fsend.at[k], frecv.at[q], re_s.at[k], re_d.at[q], box=h * 32 + 2 * k + c).wait_send()

    for e in range(4):
        mate_copy(0, e).wait_send()
        mate_copy(2, e).wait_send()
    rim_down.wait_send()
    rim_up.wait_send()


def local(
    child_pattern,
    child_parent,
    child_octant,
    child_sources,
    child_offsets,
    child_counts,
    parent_sources,
    parent_offsets,
    parent_counts,
    interp_weights,
    shift_phase,
    child_table,
    parent_table,
):
    me = lax.axis_index("box")
    h, q, c = me // 32, (me // 2) % 16, me % 2
    own = child_pattern[:, 0]
    angles = shift_phase[:, 0, :]
    cosine, sine = jnp.cos(angles), jnp.sin(angles)
    slot_row = (child_octant * PAR + child_parent - me * PAR)[None, :]
    tpar = jnp.transpose(parent_table[:, :, 0, :], (0, 2, 1))

    src = parent_sources.T
    dev = src // PAR
    hs, qs, cs = dev // 32, (dev // 2) % 16, dev % 2
    slot = (hs ^ h) * 2 + (cs ^ c)
    srow = ((slot * 16 + qs) * PAR + src % PAR) * 4
    live = jnp.arange(8, dtype=jnp.int32)[:, None] < parent_counts[None, :]
    toff = jnp.where(live, parent_offsets.T, NOFF) * 4

    rel = child_sources.T - me * 128
    pos = jnp.where(rel < 0, rel + 160, jnp.where(rel < 128, rel, rel + 32)).astype(F32)
    alive = jnp.arange(8, dtype=jnp.int32)[:, None] < child_counts[None, :]
    off = jnp.where(alive, child_offsets.T, OFFPAD).astype(F32)
    ctab = jnp.transpose(child_table[:, :, 0, :], (1, 0, 2)).reshape(NOFF, 1024)
    ctab = jnp.pad(ctab, ((0, OFFPAD - NOFF), (0, 0)))

    dma = pltpu.SemaphoreType.DMA
    vm = pl.BlockSpec(memory_space=pltpu.VMEM)
    sm = pl.BlockSpec(memory_space=pltpu.SMEM)
    out = pl.pallas_call(
        whole,
        out_shape=jax.ShapeDtypeStruct((2, KCG, 128), BF16),
        in_specs=[sm] * 2 + [vm] * 9,
        out_specs=vm,
        scratch_shapes=[
            pltpu.VMEM((2, RIM, 128), BF16),
            pltpu.VMEM((2, RIM, 128), BF16),
            pltpu.VMEM((2, PAR, KCG), BF16),
            pltpu.VMEM((2, PAR, KCG), BF16),
            pltpu.VMEM((2, 2, PAR, KCG), BF16),
            pltpu.VMEM((2, PAR, OFFPAD), BF16),
            pltpu.VMEM((3, 2, PAR, OFFPAD), BF16),
            pltpu.VMEM((2 * SLOTS, KCG), BF16),
            pltpu.VMEM((2 * SLOTS, 2 * RIM), BF16),
            pltpu.VMEM((2 * SLOTS, KPG), F32),
            pltpu.VMEM((16, 2, PAR, 128), BF16),
            pltpu.VMEM((4, 16, 2, PAR, 128), BF16),
            pltpu.VMEM((8192, 128), F32),
            pltpu.VMEM((2, 128, OFFPAD), F32),
            pltpu.VMEM((4 * OFFPAD, 128), F32),
            pltpu.VMEM((4 * PAR, 128), F32),
            pltpu.VMEM((16, 2, PAR, 128), BF16),
            pltpu.VMEM((16, 2, PAR, 128), BF16),
            pltpu.VMEM((2, SLOTS, KPG), BF16),
            pltpu.VMEM((256, KPG), BF16),
            pltpu.VMEM((2, 2, RIM, 128), BF16),
            pltpu.VMEM((2, RIM, 128), BF16),
            pltpu.VMEM((2, RIM, 128), BF16),
            pltpu.VMEM((2, KCG, 128), F32),
            pltpu.VMEM((1024, 256), BF16),
            pltpu.VMEM((1024, OFFPAD), BF16),
        ]
        + [dma((n,)) for n in (2, 2, 2, 2, 3, 3, 16, 16, 16, 16, 8, 8, 16, 16, 2, 2)],
        compiler_params=pltpu.CompilerParams(
            collective_id=0, has_side_effects=True, vmem_limit_bytes=60000 * 1024
        ),
    )(srow, toff, own, interp_weights, cosine, sine, slot_row, tpar, ctab, pos, off)
    return out[:, None]


def solution(mesh):
    return jax.shard_map(
        local,
        mesh=mesh,
        in_specs=(
            P(None, "samp", None, "box"),
            P("box"),
            P("box"),
            P("box", None),
            P("box", None),
            P("box"),
            P(),
            P(),
            P(),
            P(),
            P(None, "samp", None),
            P(None, None, "samp", None),
            P(None, None, "samp", "box"),
        ),
        out_specs=P(None, "samp", None, "box"),
        check_vma=False,
    )
```

```python
import functools

import jax
import jax.numpy as jnp
from jax import lax
from jax.experimental import pallas as pl
from jax.experimental.pallas import tpu as pltpu
from jax.sharding import PartitionSpec as P

PAR = 32
KCG = 512
KPG = 2048
RIM = 64
NOFF = 316
OFFPAD = 384
SLOTS = 256
F32 = jnp.float32
BF16 = jnp.bfloat16
NT = (((1,), (1,)), ((), ()))


def slot_matrix(slot_row):
    rows = lax.broadcasted_iota(jnp.int32, (SLOTS, 128), 0)
    return (rows == slot_row).astype(F32).astype(BF16)


def low_lanes(rows):
    return lax.broadcasted_iota(jnp.int32, (rows, 128), 1) < 64


def copy_to(src, dst, send_sem, recv_sem, **device):
    return pltpu.make_async_remote_copy(
        src_ref=src,
        dst_ref=dst,
        send_sem=send_sem,
        recv_sem=recv_sem,
        device_id=device,
        device_id_type=pl.DeviceIdType.MESH,
    )


def near_lists(own, before, after, table, post, offt, near, ohs, oht):
    srow = lax.broadcasted_iota(jnp.int32, (128, 256), 1).astype(F32)
    trow = lax.broadcasted_iota(jnp.int32, (128, OFFPAD), 1).astype(F32)
    for m in range(8):
        ohs[m * 128 : (m + 1) * 128] = (post[:, m : m + 1] == srow).astype(F32).astype(BF16)
        oht[m * 128 : (m + 1) * 128] = (offt[:, m : m + 1] == trow).astype(F32).astype(BF16)
    for n in range(2):
        at = 256 * n
        ts, ps = [], []
        for r in range(2):
            ts.append(jnp.dot(oht[...], table[:, r * 512 + at : r * 512 + at + 256], preferred_element_type=F32))
            halo = jnp.concatenate([before[r, :, at : at + 256], after[r, :, at : at + 256]], axis=0)
            p = lax.dot_general(ohs[:, 0:128], own[r, at : at + 256], NT, preferred_element_type=F32)
            ps.append(p + jnp.dot(ohs[:, 128:192], halo, preferred_element_type=F32))
        re = ts[0] * ps[0] - ts[1] * ps[1]
        im = ts[0] * ps[1] + ts[1] * ps[0]
        for r, v in enumerate((re, im)):
            total = v[0:128]
            for m in range(1, 8):
                total = total + v[m * 128 : (m + 1) * 128]
            near[r, at : at + 256] = total.T


def whole(
    own_h, w_h, phase_h, tpar_h, ctab_h, cpar, coct, csrc, coff, ccnt, psrc, poff, pcnt,
    out,
    own, w, phase, tpar, craw, ctab, cflat, cosine, sine,
    halo_l, halo_r, box_b, box_a, bsend, tsend, tparts, xown, xrim, ybuf, send, prec,
    sall, oall, smine, omine, ohx, oho, ohp, gown, tgat, tmat, tt,
    fsend, frecv, lslot, lsel, rsend, rim_lo, rim_hi, near, ohs, oht,
    in_s, halo_s, halo_d, box_s, box_d, t_s, t_d, pl_s, pl_d, cr_s, cr_d, co_s, co_d, re_s, re_d, rim_s, rim_d,
):
    d = lax.axis_index("box")
    g = lax.axis_index("samp")
    h, q, c = d // 32, (d // 2) % 16, d % 2
    gup, gdown = (g + 1) % 8, (g + 7) % 8
    mate = d + 1 - 2 * c
    far_half = (1 - h) * 32

    loads = [
        pltpu.make_async_copy(a, b, in_s.at[i])
        for i, (a, b) in enumerate(((own_h, own), (tpar_h, tpar), (phase_h, phase), (w_h, w), (ctab_h, craw)))
    ]
    for load in loads:
        load.start()

    barrier = pltpu.get_barrier_semaphore()

    def greet(**device):
        pl.semaphore_signal(barrier, inc=1, device_id=device, device_id_type=pl.DeviceIdType.MESH)

    for k in range(16):
        greet(box=far_half + 2 * k + c)
    greet(samp=gup)
    greet(samp=gdown)
    for k in range(16):

        @pl.when(q != k)
        def _():
            greet(box=h * 32 + 2 * k + c)

    greet(box=mate)

    @pl.when(d < 63)
    def _():
        greet(box=d + 1)

    @pl.when(d > 0)
    def _():
        greet(box=d - 1)

    @pl.when(d == 0)
    def _():
        box_b[...] = jnp.zeros_like(box_b)

    @pl.when(d == 63)
    def _():
        box_a[...] = jnp.zeros_like(box_a)

    slots = lax.broadcasted_iota(jnp.int32, (8, 128), 0)
    for i in range(16):
        cols = pl.ds(128 * i, 128)
        s = psrc[:, cols]
        slot = ((lax.shift_right_logical(s, 10) ^ h) * 2) | ((lax.shift_right_logical(s, 5) & 1) ^ c)
        at = slot * 512 + (lax.shift_right_logical(s, 6) & 15) * 32 + (s & 31)
        sall[128 * i : 128 * i + 128] = at.astype(F32).T
        o = jnp.where(slots < pcnt[:, cols], poff[:, cols], OFFPAD)
        oall[128 * i : 128 * i + 128] = o.astype(F32).T
    for k in range(16):
        rows = pl.ds(pl.multiple_of(h * 1024 + 64 * k + 32 * c, 32), 32)
        smine[32 * k : 32 * k + 32] = sall[rows]
        omine[32 * k : 32 * k + 32] = oall[rows]

    loads[0].wait()
    pick = lax.broadcasted_iota(jnp.int32, (PAR, 128), 0)
    lane = lax.broadcasted_iota(jnp.int32, (PAR, 128), 1)
    last = (pick + 96 == lane).astype(F32).astype(BF16)
    first = (pick == lane).astype(F32).astype(BF16)
    for r in range(2):
        bsend[0, r] = lax.dot_general(last, own[r], NT, preferred_element_type=F32).astype(BF16)
        bsend[1, r] = lax.dot_general(first, own[r], NT, preferred_element_type=F32).astype(BF16)
    loads[1].wait()
    tsend[...] = jnp.zeros_like(tsend)
    tsend[:, :, 0:NOFF] = tpar[...]
    sel = slot_matrix(coct[...] * PAR + cpar[...] - d * PAR)
    for r in range(2):
        xown[r * SLOTS : (r + 1) * SLOTS] = lax.dot_general(
            sel, own[r], NT, preferred_element_type=F32
        ).astype(BF16)
    loads[2].wait()
    for o in range(8):
        cosine[o : o + 1] = phase[o]
    angles = cosine[...]
    cosine[...] = jnp.cos(angles)
    sine[...] = jnp.sin(angles)
    loads[3].wait()
    for t in range(8):
        ybuf[:, 256 * t : 256 * t + 256] = jnp.dot(
            xown[...], w[RIM : RIM + KCG, 256 * t : 256 * t + 256], preferred_element_type=F32
        )
    wide = lax.broadcasted_iota(jnp.int32, (128, 1024), 1).astype(F32)

    def cross_hot(b, carry):
        rows = pl.ds(pl.multiple_of(128 * b, 128), 128)
        for m in range(8):
            ohx[pl.ds(pl.multiple_of(1024 * b, 1024) + 128 * m, 128)] = (
                (smine[rows, m : m + 1] - 1024.0 == wide).astype(F32).astype(BF16)
            )
        return carry

    lax.fori_loop(0, 4, cross_hot, 0)

    pl.semaphore_wait(barrier, 34 + (d < 63).astype(jnp.int32) + (d > 0).astype(jnp.int32))

    to_up = copy_to(own.at[:, KCG - RIM :], halo_l, halo_s.at[0], halo_d.at[0], samp=gup)
    to_down = copy_to(own.at[:, :RIM], halo_r, halo_s.at[1], halo_d.at[1], samp=gdown)
    to_up.start()
    to_down.start()
    t_far = copy_to(tsend, tparts.at[1], t_s.at[0], t_d.at[0], box=far_half + 2 * q + c)
    t_mate = copy_to(tsend, tparts.at[0], t_s.at[1], t_d.at[1], box=mate)
    box_up = copy_to(bsend.at[0], box_b, box_s.at[0], box_d.at[0], box=d + 1)
    box_down = copy_to(bsend.at[1], box_a, box_s.at[1], box_d.at[1], box=d - 1)

    @pl.when(d < 63)
    def _():
        box_up.start()

    @pl.when(d > 0)
    def _():
        box_down.start()

    t_far.start()
    t_mate.start()

    to_up.wait_recv()
    to_down.wait_recv()
    for r in range(2):
        rows = pl.ds(r * SLOTS, SLOTS)
        xrim[rows, 0:RIM] = lax.dot_general(sel, halo_l[r], NT, preferred_element_type=F32).astype(BF16)
        xrim[rows, RIM : 2 * RIM] = lax.dot_general(sel, halo_r[r], NT, preferred_element_type=F32).astype(BF16)
    low = low_lanes(PAR)

    def plane_copy(k):
        return copy_to(send.at[k], prec.at[0, q], pl_s.at[k], pl_d.at[q], box=h * 32 + 2 * k + c)

    def cross_copy(k):
        return copy_to(send.at[k], prec.at[2, q], cr_s.at[k], cr_d.at[q], box=far_half + 2 * k + c)

    for t in range(4):
        parts = []
        for half in range(2):
            at = half * 1024 + 256 * t
            rim_w = jnp.concatenate([w[0:RIM, at : at + 256], w[RIM + KCG :, at : at + 256]], axis=0)
            y = ybuf[:, at : at + 256] + jnp.dot(xrim[...], rim_w, preferred_element_type=F32)
            cc = cosine[:, at : at + 256]
            ss = sine[:, at : at + 256]
            re = im = None
            for o in range(8):
                yr = y[o * PAR : (o + 1) * PAR]
                yi = y[SLOTS + o * PAR : SLOTS + (o + 1) * PAR]
                co, so = cc[o : o + 1], ss[o : o + 1]
                tr = yr * co - yi * so
                ti = yr * so + yi * co
                re = tr if re is None else re + tr
                im = ti if im is None else im + ti
            parts.append((re, im))
        for u in range(2):
            for r in range(2):
                a = parts[0][r][:, 128 * u : 128 * u + 128]
                b = parts[1][r][:, 128 * u : 128 * u + 128]
                at = 128 * r
                send[4 * t + 2 * u, :, at : at + 128] = jnp.where(low, a, pltpu.roll(b, 64, 1)).astype(BF16)
                send[4 * t + 2 * u + 1, :, at : at + 128] = jnp.where(low, pltpu.roll(a, 64, 1), b).astype(BF16)
        for k in range(4 * t, 4 * t + 4):
            cross_copy(k).start()

            @pl.when(q != k)
            def _():
                plane_copy(k).start()

    prec[0, q] = send[q]

    def from_plane(k):
        return copy_to(send.at[k], prec.at[0, k], pl_s.at[k], pl_d.at[k], box=mate)

    def from_cross(k):
        return copy_to(send.at[k], prec.at[2, k], cr_s.at[k], cr_d.at[k], box=mate)

    def mate_copy(j, e):
        return copy_to(
            prec.at[j, pl.ds(4 * e, 4)], prec.at[j + 1, pl.ds(4 * e, 4)],
            co_s.at[2 * j + e], co_d.at[2 * j + e], box=mate,
        )

    for e in range(4):
        for k in range(4 * e, 4 * e + 4):

            @pl.when(q != k)
            def _():
                from_plane(k).wait_recv()

        mate_copy(0, e).start()

    loads[4].wait()
    ctab[NOFF - 12 :] = jnp.zeros((OFFPAD - NOFF + 12, 2 * KCG), BF16)
    for n in range(4):
        cflat[...] = craw[:, :, 128 * n : 128 * n + 128].astype(F32).reshape(2 * NOFF, 128)
        for r in range(2):
            at = KCG * r + 128 * n
            ctab[0:NOFF, at : at + 128] = cflat[pl.ds(r, NOFF, stride=2), :].astype(BF16)

    rel = csrc[...] - d * 128
    pos = jnp.where(rel < 0, rel + 160, jnp.where(rel < 128, rel, rel + 32)).astype(F32)
    off = jnp.where(slots < ccnt[...], coff[...], OFFPAD).astype(F32)

    @pl.when(d > 0)
    def _():
        copy_to(bsend.at[0], box_b, box_s.at[0], box_d.at[0], box=mate).wait_recv()

    @pl.when(d < 63)
    def _():
        copy_to(bsend.at[1], box_a, box_s.at[1], box_d.at[1], box=mate).wait_recv()

    near_lists(own, box_b, box_a, ctab, pos.T, off.T, near, ohs, oht)

    t_far.wait_recv()
    t_second = copy_to(tparts.at[1], tparts.at[2], t_s.at[2], t_d.at[2], box=mate)
    t_second.start()
    t_mate.wait_recv()
    t_second.wait_recv()
    for j in range(4):
        hs = h + (j // 2) - 2 * h * (j // 2)
        cs = c + (j % 2) - 2 * c * (j % 2)
        at = pl.multiple_of(64 * hs + 32 * cs, 32)
        for r in range(2):
            tt[r, pl.ds(at, 32), :] = (tsend[r] if j == 0 else tparts[j - 1, r]).astype(F32)
    for r in range(2):
        tmat[:, 128 * r : 128 * r + 128] = tt[r].T.astype(BF16)

    narrow = lax.broadcasted_iota(jnp.int32, (128, OFFPAD), 1).astype(F32)
    for e in range(4):
        mate_copy(0, e).wait_recv()

    def own_half(b, carry):
        rows = pl.ds(pl.multiple_of(128 * b, 128), 128)
        block = pl.ds(pl.multiple_of(1024 * b, 1024), 1024)
        for m in range(8):
            oho[128 * m : 128 * m + 128] = (smine[rows, m : m + 1] == wide).astype(F32).astype(BF16)
            ohp[128 * m : 128 * m + 128] = (omine[rows, m : m + 1] == narrow).astype(F32).astype(BF16)
        gown[block] = jnp.dot(oho[...], prec[0:2].reshape(1024, 256), preferred_element_type=F32)
        tgat[block] = jnp.dot(ohp[...], tmat[...], preferred_element_type=F32)
        return carry

    lax.fori_loop(0, 4, own_half, 0)

    for e in range(4):
        for k in range(4 * e, 4 * e + 4):
            from_cross(k).wait_recv()
        mate_copy(2, e).start()
    for e in range(4):
        mate_copy(2, e).wait_recv()

    def return_copy(k):
        return copy_to(fsend.at[k], frecv.at[q], re_s.at[k], re_d.at[q], box=h * 32 + 2 * k + c)

    def targets(b, carry):
        block = pl.ds(pl.multiple_of(1024 * b, 1024), 1024)
        p = gown[block] + jnp.dot(ohx[block], prec[2:4].reshape(1024, 256), preferred_element_type=F32)
        tc = tgat[block]
        re = im = None
        for m in range(8):
            rows = slice(128 * m, 128 * m + 128)
            pr, pi = p[rows, 0:128], p[rows, 128:256]
            tr, ti = tc[rows, 0:128], tc[rows, 128:256]
            x = tr * pr - ti * pi
            y = tr * pi + ti * pr
            re = x if re is None else re + x
            im = y if im is None else im + y
        for e in range(4):
            k = 4 * b + e
            fsend[k, :, 0:128] = re[32 * e : 32 * e + 32].astype(BF16)
            fsend[k, :, 128:256] = im[32 * e : 32 * e + 32].astype(BF16)

            @pl.when(q != k)
            def _():
                return_copy(k).start()

        return carry

    lax.fori_loop(0, 4, targets, 0)
    frecv[q] = fsend[q]

    for t in range(8):
        for k in range(2 * t, 2 * t + 2):

            @pl.when(q != k)
            def _():
                copy_to(fsend.at[k], frecv.at[k], re_s.at[k], re_d.at[k], box=mate).wait_recv()

        tiles = []
        for r in range(2):
            a = frecv[2 * t, :, 128 * r : 128 * r + 128].astype(F32)
            b = frecv[2 * t + 1, :, 128 * r : 128 * r + 128].astype(F32)
            tiles.append((jnp.where(low, a, pltpu.roll(b, 64, 1)), jnp.where(low, pltpu.roll(a, 64, 1), b)))
        for half in range(2):
            fr, fi = tiles[0][half], tiles[1][half]
            at = half * 1024 + 128 * t
            for o in range(8):
                co = cosine[o : o + 1, at : at + 128]
                so = sine[o : o + 1, at : at + 128]
                lslot[0, o * PAR : (o + 1) * PAR, at : at + 128] = (fr * co + fi * so).astype(BF16)
                lslot[1, o * PAR : (o + 1) * PAR, at : at + 128] = (fi * co - fr * so).astype(BF16)
    for r in range(2):
        lsel[r * 128 : (r + 1) * 128] = lax.dot_general(
            sel, lslot[r], (((0,), (0,)), ((), ())), preferred_element_type=F32
        ).astype(BF16)

    lows = lax.dot_general(w[0:RIM], lsel[...], NT, preferred_element_type=F32)
    highs = lax.dot_general(w[RIM + KCG :], lsel[...], NT, preferred_element_type=F32)
    for r in range(2):
        rsend[0, r] = lows[:, r * 128 : (r + 1) * 128].astype(BF16)
        rsend[1, r] = highs[:, r * 128 : (r + 1) * 128].astype(BF16)
    rim_down = copy_to(rsend.at[0], rim_hi, rim_s.at[0], rim_d.at[0], samp=gdown)
    rim_up = copy_to(rsend.at[1], rim_lo, rim_s.at[1], rim_d.at[1], samp=gup)
    rim_down.start()
    rim_up.start()
    mids = lax.dot_general(w[RIM : RIM + KCG], lsel[...], NT, preferred_element_type=F32)
    for r in range(2):
        mid = mids[:, r * 128 : (r + 1) * 128].astype(BF16).astype(F32)
        out[r, RIM : KCG - RIM] = (near[r, RIM : KCG - RIM] + mid[RIM : KCG - RIM]).astype(BF16)
        near[r, 0:RIM] = near[r, 0:RIM] + mid[0:RIM]
        near[r, KCG - RIM :] = near[r, KCG - RIM :] + mid[KCG - RIM :]
    rim_down.wait_recv()
    rim_up.wait_recv()
    for r in range(2):
        out[r, 0:RIM] = (near[r, 0:RIM] + rim_lo[r].astype(F32)).astype(BF16)
        out[r, KCG - RIM :] = (near[r, KCG - RIM :] + rim_hi[r].astype(F32)).astype(BF16)

    to_up.wait_send()
    to_down.wait_send()
    t_far.wait_send()
    t_mate.wait_send()
    t_second.wait_send()

    @pl.when(d < 63)
    def _():
        box_up.wait_send()

    @pl.when(d > 0)
    def _():
        box_down.wait_send()

    for k in range(16):
        cross_copy(k).wait_send()

        @pl.when(q != k)
        def _():
            plane_copy(k).wait_send()
            return_copy(k).wait_send()

    for e in range(4):
        mate_copy(0, e).wait_send()
        mate_copy(2, e).wait_send()
    rim_down.wait_send()
    rim_up.wait_send()


def local(
    child_pattern,
    child_parent,
    child_octant,
    child_sources,
    child_offsets,
    child_counts,
    parent_sources,
    parent_offsets,
    parent_counts,
    interp_weights,
    shift_phase,
    child_table,
    parent_table,
):
    dma = pltpu.SemaphoreType.DMA
    vm = pl.BlockSpec(memory_space=pltpu.VMEM)
    anywhere = pl.BlockSpec(memory_space=pl.ANY)
    out = pl.pallas_call(
        whole,
        out_shape=jax.ShapeDtypeStruct((2, KCG, 128), BF16),
        in_specs=[anywhere] * 5 + [vm] * 8,
        out_specs=vm,
        scratch_shapes=[
            pltpu.VMEM((2, KCG, 128), BF16),
            pltpu.VMEM((KCG + 2 * RIM, KPG), BF16),
            pltpu.VMEM((8, 1, KPG), F32),
            pltpu.VMEM((2, PAR, NOFF), BF16),
            pltpu.VMEM((NOFF, 2, KCG), BF16),
            pltpu.VMEM((OFFPAD, 2 * KCG), BF16),
            pltpu.VMEM((2 * NOFF, 128), F32),
            pltpu.VMEM((8, KPG), F32),
            pltpu.VMEM((8, KPG), F32),
            pltpu.VMEM((2, RIM, 128), BF16),
            pltpu.VMEM((2, RIM, 128), BF16),
            pltpu.VMEM((2, PAR, KCG), BF16),
            pltpu.VMEM((2, PAR, KCG), BF16),
            pltpu.VMEM((2, 2, PAR, KCG), BF16),
            pltpu.VMEM((2, PAR, OFFPAD), BF16),
            pltpu.VMEM((3, 2, PAR, OFFPAD), BF16),
            pltpu.VMEM((2 * SLOTS, KCG), BF16),
            pltpu.VMEM((2 * SLOTS, 2 * RIM), BF16),
            pltpu.VMEM((2 * SLOTS, KPG), F32),
            pltpu.VMEM((16, PAR, 256), BF16),
            pltpu.VMEM((4, 16, PAR, 256), BF16),
            pltpu.VMEM((2048, 8), F32),
            pltpu.VMEM((2048, 8), F32),
            pltpu.VMEM((512, 8), F32),
            pltpu.VMEM((512, 8), F32),
            pltpu.VMEM((4096, 1024), BF16),
            pltpu.VMEM((1024, 1024), BF16),
            pltpu.VMEM((1024, OFFPAD), BF16),
            pltpu.VMEM((4096, 256), F32),
            pltpu.VMEM((4096, 256), F32),
            pltpu.VMEM((OFFPAD, 256), BF16),
            pltpu.VMEM((2, 128, OFFPAD), F32),
            pltpu.VMEM((16, PAR, 256), BF16),
            pltpu.VMEM((16, PAR, 256), BF16),
            pltpu.VMEM((2, SLOTS, KPG), BF16),
            pltpu.VMEM((256, KPG), BF16),
            pltpu.VMEM((2, 2, RIM, 128), BF16),
            pltpu.VMEM((2, RIM, 128), BF16),
            pltpu.VMEM((2, RIM, 128), BF16),
            pltpu.VMEM((2, KCG, 128), F32),
            pltpu.VMEM((1024, 256), BF16),
            pltpu.VMEM((1024, OFFPAD), BF16),
        ]
        + [dma((n,)) for n in (5, 2, 2, 2, 2, 3, 3, 16, 16, 16, 16, 8, 8, 16, 16, 2, 2)],
        compiler_params=pltpu.CompilerParams(
            collective_id=0, has_side_effects=True, vmem_limit_bytes=60000 * 1024
        ),
    )(
        child_pattern[:, 0],
        interp_weights,
        shift_phase,
        jnp.transpose(parent_table[:, :, 0, :], (0, 2, 1)),
        jnp.transpose(child_table[:, :, 0, :], (1, 0, 2)),
        child_parent[None, :],
        child_octant[None, :],
        child_sources.T,
        child_offsets.T,
        child_counts[None, :],
        parent_sources.T,
        parent_offsets.T,
        parent_counts[None, :],
    )
    return out[:, None]


def solution(mesh):
    return jax.shard_map(
        local,
        mesh=mesh,
        in_specs=(
            P(None, "samp", None, "box"),
            P("box"),
            P("box"),
            P("box", None),
            P("box", None),
            P("box"),
            P(),
            P(),
            P(),
            P(),
            P(None, "samp", None),
            P(None, None, "samp", None),
            P(None, None, "samp", "box"),
        ),
        out_specs=P(None, "samp", None, "box"),
        check_vma=False,
    )
```

```python
import functools

import jax
import jax.numpy as jnp
from jax import lax
from jax.experimental import pallas as pl
from jax.experimental.pallas import tpu as pltpu
from jax.sharding import PartitionSpec as P

PAR = 32
KCG = 512
KPG = 2048
RIM = 64
NOFF = 316
OFFPAD = 384
SLOTS = 256
F32 = jnp.float32
BF16 = jnp.bfloat16
NT = (((1,), (1,)), ((), ()))


def slot_matrix(slot_row):
    rows = lax.broadcasted_iota(jnp.int32, (SLOTS, 128), 0)
    return (rows == slot_row).astype(F32).astype(BF16)


def low_lanes(rows):
    return lax.broadcasted_iota(jnp.int32, (rows, 128), 1) < 64


def copy_to(src, dst, send_sem, recv_sem, **device):
    return pltpu.make_async_remote_copy(
        src_ref=src,
        dst_ref=dst,
        send_sem=send_sem,
        recv_sem=recv_sem,
        device_id=device,
        device_id_type=pl.DeviceIdType.MESH,
    )


def near_lists(own, before, after, table, post, offt, near, ohs, oht):
    srow = lax.broadcasted_iota(jnp.int32, (128, 256), 1).astype(F32)
    trow = lax.broadcasted_iota(jnp.int32, (128, OFFPAD), 1).astype(F32)
    for m in range(8):
        ohs[m * 128 : (m + 1) * 128] = (post[:, m : m + 1] == srow).astype(F32).astype(BF16)
        oht[m * 128 : (m + 1) * 128] = (offt[:, m : m + 1] == trow).astype(F32).astype(BF16)
    for n in range(2):
        at = 256 * n
        ts, ps = [], []
        for r in range(2):
            ts.append(jnp.dot(oht[...], table[:, r * 512 + at : r * 512 + at + 256], preferred_element_type=F32))
            halo = jnp.concatenate([before[r, :, at : at + 256], after[r, :, at : at + 256]], axis=0)
            p = lax.dot_general(ohs[:, 0:128], own[r, at : at + 256], NT, preferred_element_type=F32)
            ps.append(p + jnp.dot(ohs[:, 128:192], halo, preferred_element_type=F32))
        re = ts[0] * ps[0] - ts[1] * ps[1]
        im = ts[0] * ps[1] + ts[1] * ps[0]
        for r, v in enumerate((re, im)):
            total = v[0:128]
            for m in range(1, 8):
                total = total + v[m * 128 : (m + 1) * 128]
            near[r, at : at + 256] = total.T


def whole(
    own_h, tpar_h, phase_h, w_h, cpar_h, coct_h, csrc_h, coff_h, ccnt_h, psrc_h, poff_h, pcnt_h, ctab_h,
    out,
    cpar, coct, csrc, coff, ccnt, psrc, poff, pcnt,
    own, w, phase, tpar, craw, ctab, cflat, cosine, sine,
    halo_l, halo_r, box_b, box_a, bsend, tsend, tparts, xown, xrim, ybuf, send, prec,
    sall, oall, smine, omine, ohx, oho, ohp, gown, tgat, tmat, tt,
    fsend, frecv, lslot, lsel, rsend, rim_lo, rim_hi, near, ohs, oht,
    in_s, halo_s, halo_d, box_s, box_d, t_s, t_d, pl_s, pl_d, cr_s, cr_d, co_s, co_d, re_s, re_d, rim_s, rim_d,
):
    d = lax.axis_index("box")
    g = lax.axis_index("samp")
    h, q, c = d // 32, (d // 2) % 16, d % 2
    gup, gdown = (g + 1) % 8, (g + 7) % 8
    mate = d + 1 - 2 * c
    far_half = (1 - h) * 32

    barrier = pltpu.get_barrier_semaphore()

    def greet(**device):
        pl.semaphore_signal(barrier, inc=1, device_id=device, device_id_type=pl.DeviceIdType.MESH)

    for k in range(16):
        greet(box=far_half + 2 * k + c)
    greet(samp=gup)
    greet(samp=gdown)
    for k in range(16):

        @pl.when(q != k)
        def _():
            greet(box=h * 32 + 2 * k + c)

    greet(box=mate)

    @pl.when(d < 63)
    def _():
        greet(box=d + 1)

    @pl.when(d > 0)
    def _():
        greet(box=d - 1)

    pairs = (
        (own_h, own), (tpar_h, tpar), (cpar_h, cpar), (coct_h, coct), (phase_h, phase), (w_h, w), (psrc_h, psrc), (poff_h, poff),
        (pcnt_h, pcnt), (csrc_h, csrc), (coff_h, coff), (ccnt_h, ccnt), (ctab_h, craw),
    )
    loads = [pltpu.make_async_copy(a, b, in_s.at[i]) for i, (a, b) in enumerate(pairs)]
    for load in loads:
        load.start()

    @pl.when(d == 0)
    def _():
        box_b[...] = jnp.zeros_like(box_b)

    @pl.when(d == 63)
    def _():
        box_a[...] = jnp.zeros_like(box_a)

    loads[0].wait()
    pl.semaphore_wait(barrier, 34 + (d < 63).astype(jnp.int32) + (d > 0).astype(jnp.int32))

    to_up = copy_to(own.at[:, KCG - RIM :], halo_l, halo_s.at[0], halo_d.at[0], samp=gup)
    to_down = copy_to(own.at[:, :RIM], halo_r, halo_s.at[1], halo_d.at[1], samp=gdown)
    to_up.start()
    to_down.start()
    loads[1].wait()
    tsend[...] = jnp.zeros_like(tsend)
    tsend[:, :, 0:NOFF] = tpar[...]
    t_far = copy_to(tsend, tparts.at[1], t_s.at[0], t_d.at[0], box=far_half + 2 * q + c)
    t_mate = copy_to(tsend, tparts.at[0], t_s.at[1], t_d.at[1], box=mate)
    t_far.start()
    t_mate.start()
    pick = lax.broadcasted_iota(jnp.int32, (PAR, 128), 0)
    lane = lax.broadcasted_iota(jnp.int32, (PAR, 128), 1)
    last = (pick + 96 == lane).astype(F32).astype(BF16)
    first = (pick == lane).astype(F32).astype(BF16)
    for r in range(2):
        bsend[0, r] = lax.dot_general(last, own[r], NT, preferred_element_type=F32).astype(BF16)
        bsend[1, r] = lax.dot_general(first, own[r], NT, preferred_element_type=F32).astype(BF16)
    box_up = copy_to(bsend.at[0], box_b, box_s.at[0], box_d.at[0], box=d + 1)
    box_down = copy_to(bsend.at[1], box_a, box_s.at[1], box_d.at[1], box=d - 1)

    @pl.when(d < 63)
    def _():
        box_up.start()

    @pl.when(d > 0)
    def _():
        box_down.start()

    for i in range(2, 6):
        loads[i].wait()
    sel = slot_matrix(coct[...] * PAR + cpar[...] - d * PAR)
    for r in range(2):
        xown[r * SLOTS : (r + 1) * SLOTS] = lax.dot_general(
            sel, own[r], NT, preferred_element_type=F32
        ).astype(BF16)
    for o in range(8):
        cosine[o : o + 1] = phase[o]
    angles = cosine[...]
    cosine[...] = jnp.cos(angles)
    sine[...] = jnp.sin(angles)
    for t in range(8):
        ybuf[:, 256 * t : 256 * t + 256] = jnp.dot(
            xown[...], w[RIM : RIM + KCG, 256 * t : 256 * t + 256], preferred_element_type=F32
        )

    to_up.wait_recv()
    to_down.wait_recv()
    for r in range(2):
        rows = pl.ds(r * SLOTS, SLOTS)
        xrim[rows, 0:RIM] = lax.dot_general(sel, halo_l[r], NT, preferred_element_type=F32).astype(BF16)
        xrim[rows, RIM : 2 * RIM] = lax.dot_general(sel, halo_r[r], NT, preferred_element_type=F32).astype(BF16)
    low = low_lanes(PAR)

    def plane_copy(k):
        return copy_to(send.at[k], prec.at[0, q], pl_s.at[k], pl_d.at[q], box=h * 32 + 2 * k + c)

    def cross_copy(k):
        return copy_to(send.at[k], prec.at[2, q], cr_s.at[k], cr_d.at[q], box=far_half + 2 * k + c)

    row, turn = q // 4, q % 4

    def shift(step, carry):
        t = (row + step) % 4
        parts = []
        for half in range(2):
            cols = pl.ds(pl.multiple_of(half * 1024 + 256 * t, 256), 256)
            rim_w = jnp.concatenate([w[0:RIM, cols], w[RIM + KCG :, cols]], axis=0)
            y = ybuf[:, cols] + jnp.dot(xrim[...], rim_w, preferred_element_type=F32)
            cc = cosine[:, cols]
            ss = sine[:, cols]
            re = im = None
            for o in range(8):
                yr = y[o * PAR : (o + 1) * PAR]
                yi = y[SLOTS + o * PAR : SLOTS + (o + 1) * PAR]
                co, so = cc[o : o + 1], ss[o : o + 1]
                tr = yr * co - yi * so
                ti = yr * so + yi * co
                re = tr if re is None else re + tr
                im = ti if im is None else im + ti
            parts.append((re, im))
        for u in range(2):
            for r in range(2):
                a = parts[0][r][:, 128 * u : 128 * u + 128]
                b = parts[1][r][:, 128 * u : 128 * u + 128]
                at = 128 * r
                send[4 * t + 2 * u, :, at : at + 128] = jnp.where(low, a, pltpu.roll(b, 64, 1)).astype(BF16)
                send[4 * t + 2 * u + 1, :, at : at + 128] = jnp.where(low, pltpu.roll(a, 64, 1), b).astype(BF16)
        for e in range(4):
            k = 4 * t + (turn + e) % 4
            cross_copy(k).start()

            @pl.when(q != k)
            def _():
                plane_copy(k).start()

        return carry

    lax.fori_loop(0, 4, shift, 0)

    prec[0, q] = send[q]

    def from_plane(k):
        return copy_to(send.at[k], prec.at[0, k], pl_s.at[k], pl_d.at[k], box=mate)

    def from_cross(k):
        return copy_to(send.at[k], prec.at[2, k], cr_s.at[k], cr_d.at[k], box=mate)

    def mate_copy(j, e):
        return copy_to(
            prec.at[j, pl.ds(4 * e, 4)], prec.at[j + 1, pl.ds(4 * e, 4)],
            co_s.at[2 * j + e], co_d.at[2 * j + e], box=mate,
        )

    def arrival(step):
        return (row + 4 - step) % 4

    for step in range(4):
        for e in range(4):
            k = 4 * arrival(step) + e

            @pl.when(q != k)
            def _():
                from_plane(k).wait_recv()

        mate_copy(0, arrival(step)).start()

    for i in range(6, 13):
        loads[i].wait()
    slots = lax.broadcasted_iota(jnp.int32, (8, 128), 0)
    for i in range(16):
        cols = pl.ds(128 * i, 128)
        s = psrc[:, cols]
        slot = ((lax.shift_right_logical(s, 10) ^ h) * 2) | ((lax.shift_right_logical(s, 5) & 1) ^ c)
        at = slot * 512 + (lax.shift_right_logical(s, 6) & 15) * 32 + (s & 31)
        sall[128 * i : 128 * i + 128] = at.astype(F32).T
        o = jnp.where(slots < pcnt[:, cols], poff[:, cols], OFFPAD)
        oall[128 * i : 128 * i + 128] = o.astype(F32).T
    for k in range(16):
        rows = pl.ds(pl.multiple_of(h * 1024 + 64 * k + 32 * c, 32), 32)
        smine[32 * k : 32 * k + 32] = sall[rows]
        omine[32 * k : 32 * k + 32] = oall[rows]

    wide = lax.broadcasted_iota(jnp.int32, (128, 1024), 1).astype(F32)

    def cross_hot(b, carry):
        rows = pl.ds(pl.multiple_of(128 * b, 128), 128)
        for m in range(8):
            ohx[pl.ds(pl.multiple_of(1024 * b, 1024) + 128 * m, 128)] = (
                (smine[rows, m : m + 1] - 1024.0 == wide).astype(F32).astype(BF16)
            )
        return carry

    lax.fori_loop(0, 4, cross_hot, 0)

    ctab[NOFF - 12 :] = jnp.zeros((OFFPAD - NOFF + 12, 2 * KCG), BF16)
    for n in range(4):
        cflat[...] = craw[:, :, 128 * n : 128 * n + 128].astype(F32).reshape(2 * NOFF, 128)
        for r in range(2):
            at = KCG * r + 128 * n
            ctab[0:NOFF, at : at + 128] = cflat[pl.ds(r, NOFF, stride=2), :].astype(BF16)

    rel = csrc[...] - d * 128
    pos = jnp.where(rel < 0, rel + 160, jnp.where(rel < 128, rel, rel + 32)).astype(F32)
    off = jnp.where(slots < ccnt[...], coff[...], OFFPAD).astype(F32)

    @pl.when(d > 0)
    def _():
        copy_to(bsend.at[0], box_b, box_s.at[0], box_d.at[0], box=mate).wait_recv()

    @pl.when(d < 63)
    def _():
        copy_to(bsend.at[1], box_a, box_s.at[1], box_d.at[1], box=mate).wait_recv()

    near_lists(own, box_b, box_a, ctab, pos.T, off.T, near, ohs, oht)

    t_far.wait_recv()
    t_second = copy_to(tparts.at[1], tparts.at[2], t_s.at[2], t_d.at[2], box=mate)
    t_second.start()
    t_mate.wait_recv()
    t_second.wait_recv()
    for j in range(4):
        hs = h + (j // 2) - 2 * h * (j // 2)
        cs = c + (j % 2) - 2 * c * (j % 2)
        at = pl.multiple_of(64 * hs + 32 * cs, 32)
        for r in range(2):
            tt[r, pl.ds(at, 32), :] = (tsend[r] if j == 0 else tparts[j - 1, r]).astype(F32)
    for r in range(2):
        tmat[:, 128 * r : 128 * r + 128] = tt[r].T.astype(BF16)

    narrow = lax.broadcasted_iota(jnp.int32, (128, OFFPAD), 1).astype(F32)
    for e in range(4):
        mate_copy(0, e).wait_recv()

    def own_half(b, carry):
        rows = pl.ds(pl.multiple_of(128 * b, 128), 128)
        block = pl.ds(pl.multiple_of(1024 * b, 1024), 1024)
        for m in range(8):
            oho[128 * m : 128 * m + 128] = (smine[rows, m : m + 1] == wide).astype(F32).astype(BF16)
            ohp[128 * m : 128 * m + 128] = (omine[rows, m : m + 1] == narrow).astype(F32).astype(BF16)
        gown[block] = jnp.dot(oho[...], prec[0:2].reshape(1024, 256), preferred_element_type=F32)
        tgat[block] = jnp.dot(ohp[...], tmat[...], preferred_element_type=F32)
        return carry

    lax.fori_loop(0, 4, own_half, 0)

    for step in range(4):
        for e in range(4):
            from_cross(4 * arrival(step) + e).wait_recv()
        mate_copy(2, arrival(step)).start()
    for e in range(4):
        mate_copy(2, e).wait_recv()

    def return_copy(k):
        return copy_to(fsend.at[k], frecv.at[q], re_s.at[k], re_d.at[q], box=h * 32 + 2 * k + c)

    def targets(step, carry):
        b = (row + step) % 4
        block = pl.ds(pl.multiple_of(1024 * b, 1024), 1024)
        p = gown[block] + jnp.dot(ohx[block], prec[2:4].reshape(1024, 256), preferred_element_type=F32)
        tc = tgat[block]
        re = im = None
        for m in range(8):
            rows = slice(128 * m, 128 * m + 128)
            pr, pi = p[rows, 0:128], p[rows, 128:256]
            tr, ti = tc[rows, 0:128], tc[rows, 128:256]
            x = tr * pr - ti * pi
            y = tr * pi + ti * pr
            re = x if re is None else re + x
            im = y if im is None else im + y
        for e in range(4):
            fsend[4 * b + e, :, 0:128] = re[32 * e : 32 * e + 32].astype(BF16)
            fsend[4 * b + e, :, 128:256] = im[32 * e : 32 * e + 32].astype(BF16)
        for e in range(4):
            k = 4 * b + (turn + e) % 4

            @pl.when(q != k)
            def _():
                return_copy(k).start()

        return carry

    lax.fori_loop(0, 4, targets, 0)
    frecv[q] = fsend[q]

    for t in range(8):
        for k in range(2 * t, 2 * t + 2):

            @pl.when(q != k)
            def _():
                copy_to(fsend.at[k], frecv.at[k], re_s.at[k], re_d.at[k], box=mate).wait_recv()

        tiles = []
        for r in range(2):
            a = frecv[2 * t, :, 128 * r : 128 * r + 128].astype(F32)
            b = frecv[2 * t + 1, :, 128 * r : 128 * r + 128].astype(F32)
            tiles.append((jnp.where(low, a, pltpu.roll(b, 64, 1)), jnp.where(low, pltpu.roll(a, 64, 1), b)))
        for half in range(2):
            fr, fi = tiles[0][half], tiles[1][half]
            at = half * 1024 + 128 * t
            for o in range(8):
                co = cosine[o : o + 1, at : at + 128]
                so = sine[o : o + 1, at : at + 128]
                lslot[0, o * PAR : (o + 1) * PAR, at : at + 128] = (fr * co + fi * so).astype(BF16)
                lslot[1, o * PAR : (o + 1) * PAR, at : at + 128] = (fi * co - fr * so).astype(BF16)
    for r in range(2):
        lsel[r * 128 : (r + 1) * 128] = lax.dot_general(
            sel, lslot[r], (((0,), (0,)), ((), ())), preferred_element_type=F32
        ).astype(BF16)

    lows = lax.dot_general(w[0:RIM], lsel[...], NT, preferred_element_type=F32)
    highs = lax.dot_general(w[RIM + KCG :], lsel[...], NT, preferred_element_type=F32)
    for r in range(2):
        rsend[0, r] = lows[:, r * 128 : (r + 1) * 128].astype(BF16)
        rsend[1, r] = highs[:, r * 128 : (r + 1) * 128].astype(BF16)
    rim_down = copy_to(rsend.at[0], rim_hi, rim_s.at[0], rim_d.at[0], samp=gdown)
    rim_up = copy_to(rsend.at[1], rim_lo, rim_s.at[1], rim_d.at[1], samp=gup)
    rim_down.start()
    rim_up.start()
    mids = lax.dot_general(w[RIM : RIM + KCG], lsel[...], NT, preferred_element_type=F32)
    for r in range(2):
        mid = mids[:, r * 128 : (r + 1) * 128].astype(BF16).astype(F32)
        out[r, RIM : KCG - RIM] = (near[r, RIM : KCG - RIM] + mid[RIM : KCG - RIM]).astype(BF16)
        near[r, 0:RIM] = near[r, 0:RIM] + mid[0:RIM]
        near[r, KCG - RIM :] = near[r, KCG - RIM :] + mid[KCG - RIM :]
    rim_down.wait_recv()
    rim_up.wait_recv()
    for r in range(2):
        out[r, 0:RIM] = (near[r, 0:RIM] + rim_lo[r].astype(F32)).astype(BF16)
        out[r, KCG - RIM :] = (near[r, KCG - RIM :] + rim_hi[r].astype(F32)).astype(BF16)

    to_up.wait_send()
    to_down.wait_send()
    t_far.wait_send()
    t_mate.wait_send()
    t_second.wait_send()

    @pl.when(d < 63)
    def _():
        box_up.wait_send()

    @pl.when(d > 0)
    def _():
        box_down.wait_send()

    for k in range(16):
        cross_copy(k).wait_send()

        @pl.when(q != k)
        def _():
            plane_copy(k).wait_send()
            return_copy(k).wait_send()

    for e in range(4):
        mate_copy(0, e).wait_send()
        mate_copy(2, e).wait_send()
    rim_down.wait_send()
    rim_up.wait_send()


def local(
    child_pattern,
    child_parent,
    child_octant,
    child_sources,
    child_offsets,
    child_counts,
    parent_sources,
    parent_offsets,
    parent_counts,
    interp_weights,
    shift_phase,
    child_table,
    parent_table,
):
    dma = pltpu.SemaphoreType.DMA
    vm = pl.BlockSpec(memory_space=pltpu.VMEM)
    anywhere = pl.BlockSpec(memory_space=pl.ANY)
    out = pl.pallas_call(
        whole,
        out_shape=pltpu.VMEM((2, KCG, 128), BF16),
        in_specs=[anywhere] * 13,
        out_specs=vm,
        scratch_shapes=[
            pltpu.VMEM((1, 128), jnp.int32),
            pltpu.VMEM((1, 128), jnp.int32),
            pltpu.VMEM((8, 128), jnp.int32),
            pltpu.VMEM((8, 128), jnp.int32),
            pltpu.VMEM((1, 128), jnp.int32),
            pltpu.VMEM((8, 2048), jnp.int32),
            pltpu.VMEM((8, 2048), jnp.int32),
            pltpu.VMEM((1, 2048), jnp.int32),
            pltpu.VMEM((2, KCG, 128), BF16),
            pltpu.VMEM((KCG + 2 * RIM, KPG), BF16),
            pltpu.VMEM((8, 1, KPG), F32),
            pltpu.VMEM((2, PAR, NOFF), BF16),
            pltpu.VMEM((NOFF, 2, KCG), BF16),
            pltpu.VMEM((OFFPAD, 2 * KCG), BF16),
            pltpu.VMEM((2 * NOFF, 128), F32),
            pltpu.VMEM((8, KPG), F32),
            pltpu.VMEM((8, KPG), F32),
            pltpu.VMEM((2, RIM, 128), BF16),
            pltpu.VMEM((2, RIM, 128), BF16),
            pltpu.VMEM((2, PAR, KCG), BF16),
            pltpu.VMEM((2, PAR, KCG), BF16),
            pltpu.VMEM((2, 2, PAR, KCG), BF16),
            pltpu.VMEM((2, PAR, OFFPAD), BF16),
            pltpu.VMEM((3, 2, PAR, OFFPAD), BF16),
            pltpu.VMEM((2 * SLOTS, KCG), BF16),
            pltpu.VMEM((2 * SLOTS, 2 * RIM), BF16),
            pltpu.VMEM((2 * SLOTS, KPG), F32),
            pltpu.VMEM((16, PAR, 256), BF16),
            pltpu.VMEM((4, 16, PAR, 256), BF16),
            pltpu.VMEM((2048, 8), F32),
            pltpu.VMEM((2048, 8), F32),
            pltpu.VMEM((512, 8), F32),
            pltpu.VMEM((512, 8), F32),
            pltpu.VMEM((4096, 1024), BF16),
            pltpu.VMEM((1024, 1024), BF16),
            pltpu.VMEM((1024, OFFPAD), BF16),
            pltpu.VMEM((4096, 256), F32),
            pltpu.VMEM((4096, 256), F32),
            pltpu.VMEM((OFFPAD, 256), BF16),
            pltpu.VMEM((2, 128, OFFPAD), F32),
            pltpu.VMEM((16, PAR, 256), BF16),
            pltpu.VMEM((16, PAR, 256), BF16),
            pltpu.VMEM((2, SLOTS, KPG), BF16),
            pltpu.VMEM((256, KPG), BF16),
            pltpu.VMEM((2, 2, RIM, 128), BF16),
            pltpu.VMEM((2, RIM, 128), BF16),
            pltpu.VMEM((2, RIM, 128), BF16),
            pltpu.VMEM((2, KCG, 128), F32),
            pltpu.VMEM((1024, 256), BF16),
            pltpu.VMEM((1024, OFFPAD), BF16),
        ]
        + [dma((n,)) for n in (13, 2, 2, 2, 2, 3, 3, 16, 16, 16, 16, 8, 8, 16, 16, 2, 2)],
        compiler_params=pltpu.CompilerParams(
            collective_id=0, has_side_effects=True, vmem_limit_bytes=60000 * 1024
        ),
    )(
        child_pattern[:, 0],
        jnp.transpose(parent_table[:, :, 0, :], (0, 2, 1)),
        shift_phase,
        interp_weights,
        child_parent[None, :],
        child_octant[None, :],
        child_sources.T,
        child_offsets.T,
        child_counts[None, :],
        parent_sources.T,
        parent_offsets.T,
        parent_counts[None, :],
        jnp.transpose(child_table[:, :, 0, :], (1, 0, 2)),
    )
    return out[:, None]


def solution(mesh):
    return jax.shard_map(
        local,
        mesh=mesh,
        in_specs=(
            P(None, "samp", None, "box"),
            P("box"),
            P("box"),
            P("box", None),
            P("box", None),
            P("box"),
            P(),
            P(),
            P(),
            P(),
            P(None, "samp", None),
            P(None, None, "samp", None),
            P(None, None, "samp", "box"),
        ),
        out_specs=P(None, "samp", None, "box"),
        check_vma=False,
    )
```

```python
import functools

import jax
import jax.numpy as jnp
from jax import lax
from jax.experimental import pallas as pl
from jax.experimental.pallas import tpu as pltpu
from jax.sharding import PartitionSpec as P

PAR = 32
KCG = 512
KPG = 2048
RIM = 64
NOFF = 316
OFFPAD = 384
SLOTS = 256
F32 = jnp.float32
BF16 = jnp.bfloat16
NT = (((1,), (1,)), ((), ()))


def slot_matrix(slot_row):
    rows = lax.broadcasted_iota(jnp.int32, (SLOTS, 128), 0)
    return (rows == slot_row).astype(F32).astype(BF16)


def low_lanes(rows):
    return lax.broadcasted_iota(jnp.int32, (rows, 128), 1) < 64


def copy_to(src, dst, send_sem, recv_sem, **device):
    return pltpu.make_async_remote_copy(
        src_ref=src,
        dst_ref=dst,
        send_sem=send_sem,
        recv_sem=recv_sem,
        device_id=device,
        device_id_type=pl.DeviceIdType.MESH,
    )


def near_lists(own, before, after, table, post, offt, near, ohs, oht):
    srow = lax.broadcasted_iota(jnp.int32, (128, 256), 1).astype(F32)
    trow = lax.broadcasted_iota(jnp.int32, (128, OFFPAD), 1).astype(F32)
    for m in range(8):
        ohs[m * 128 : (m + 1) * 128] = (post[:, m : m + 1] == srow).astype(F32).astype(BF16)
        oht[m * 128 : (m + 1) * 128] = (offt[:, m : m + 1] == trow).astype(F32).astype(BF16)
    for n in range(2):
        at = 256 * n
        ts, ps = [], []
        for r in range(2):
            ts.append(jnp.dot(oht[...], table[:, r * 512 + at : r * 512 + at + 256], preferred_element_type=F32))
            halo = jnp.concatenate([before[r, :, at : at + 256], after[r, :, at : at + 256]], axis=0)
            p = lax.dot_general(ohs[:, 0:128], own[r, at : at + 256], NT, preferred_element_type=F32)
            ps.append(p + jnp.dot(ohs[:, 128:192], halo, preferred_element_type=F32))
        re = ts[0] * ps[0] - ts[1] * ps[1]
        im = ts[0] * ps[1] + ts[1] * ps[0]
        for r, v in enumerate((re, im)):
            total = v[0:128]
            for m in range(1, 8):
                total = total + v[m * 128 : (m + 1) * 128]
            near[r, at : at + 256] = total.T


def whole(
    own_h, tpar_h, phase_h, w_h, cpar_h, coct_h, csrc_h, coff_h, ccnt_h, psrc_h, poff_h, pcnt_h, ctab_h,
    out,
    cpar, coct, csrc, coff, ccnt, psrc, poff, pcnt,
    own, w, phase, tpar, craw, ctab, cflat, cosine, sine,
    halo_l, halo_r, box_b, box_a, bsend, tsend, tparts, xown, xrim, ybuf, send, prec,
    sall, oall, smine, omine, ohx, oho, ohp, gown, tgat, tmat, tt,
    fsend, frecv, lslot, lsel, rsend, rim_lo, rim_hi, near, ohs, oht,
    in_s, halo_s, halo_d, box_s, box_d, t_s, t_d, pl_s, pl_d, cr_s, cr_d, co_s, co_d, re_s, re_d, rim_s, rim_d,
):
    d = lax.axis_index("box")
    g = lax.axis_index("samp")
    h, q, c = d // 32, (d // 2) % 16, d % 2
    gup, gdown = (g + 1) % 8, (g + 7) % 8
    mate = d + 1 - 2 * c
    far_half = (1 - h) * 32

    barrier = pltpu.get_barrier_semaphore()

    def greet(**device):
        pl.semaphore_signal(barrier, inc=1, device_id=device, device_id_type=pl.DeviceIdType.MESH)

    for k in range(16):
        greet(box=far_half + 2 * k + c)
    greet(samp=gup)
    greet(samp=gdown)
    for k in range(16):

        @pl.when(q != k)
        def _():
            greet(box=h * 32 + 2 * k + c)

    greet(box=mate)

    @pl.when(d < 63)
    def _():
        greet(box=d + 1)

    @pl.when(d > 0)
    def _():
        greet(box=d - 1)

    pairs = (
        (own_h, own), (tpar_h, tpar), (cpar_h, cpar), (coct_h, coct), (phase_h, phase), (w_h, w), (psrc_h, psrc), (poff_h, poff),
        (pcnt_h, pcnt), (csrc_h, csrc), (coff_h, coff), (ccnt_h, ccnt), (ctab_h, craw),
    )
    loads = [pltpu.make_async_copy(a, b, in_s.at[i]) for i, (a, b) in enumerate(pairs)]
    for load in loads:
        load.start()

    @pl.when(d == 0)
    def _():
        box_b[...] = jnp.zeros_like(box_b)

    @pl.when(d == 63)
    def _():
        box_a[...] = jnp.zeros_like(box_a)

    loads[0].wait()
    loads[1].wait()
    tsend[...] = jnp.zeros_like(tsend)
    tsend[:, :, 0:NOFF] = tpar[...]
    pick = lax.broadcasted_iota(jnp.int32, (PAR, 128), 0)
    lane = lax.broadcasted_iota(jnp.int32, (PAR, 128), 1)
    last = (pick + 96 == lane).astype(F32).astype(BF16)
    first = (pick == lane).astype(F32).astype(BF16)
    for r in range(2):
        bsend[0, r] = lax.dot_general(last, own[r], NT, preferred_element_type=F32).astype(BF16)
        bsend[1, r] = lax.dot_general(first, own[r], NT, preferred_element_type=F32).astype(BF16)
    for i in range(2, 6):
        loads[i].wait()
    sel = slot_matrix(coct[...] * PAR + cpar[...] - d * PAR)
    for r in range(2):
        xown[r * SLOTS : (r + 1) * SLOTS] = lax.dot_general(
            sel, own[r], NT, preferred_element_type=F32
        ).astype(BF16)
    for o in range(8):
        cosine[o : o + 1] = phase[o]
    angles = cosine[...]
    cosine[...] = jnp.cos(angles)
    sine[...] = jnp.sin(angles)
    for t in range(8):
        ybuf[:, 256 * t : 256 * t + 256] = jnp.dot(
            xown[...], w[RIM : RIM + KCG, 256 * t : 256 * t + 256], preferred_element_type=F32
        )

    pl.semaphore_wait(barrier, 34 + (d < 63).astype(jnp.int32) + (d > 0).astype(jnp.int32))

    to_up = copy_to(own.at[:, KCG - RIM :], halo_l, halo_s.at[0], halo_d.at[0], samp=gup)
    to_down = copy_to(own.at[:, :RIM], halo_r, halo_s.at[1], halo_d.at[1], samp=gdown)

    @pl.when(g != 7)
    def _():
        to_up.start()

    to_down.start()

    @pl.when(g == 7)
    def _():
        to_up.start()

    t_far = copy_to(tsend, tparts.at[1], t_s.at[0], t_d.at[0], box=far_half + 2 * q + c)
    t_mate = copy_to(tsend, tparts.at[0], t_s.at[1], t_d.at[1], box=mate)
    t_far.start()
    t_mate.start()
    box_up = copy_to(bsend.at[0], box_b, box_s.at[0], box_d.at[0], box=d + 1)
    box_down = copy_to(bsend.at[1], box_a, box_s.at[1], box_d.at[1], box=d - 1)

    @pl.when(d < 63)
    def _():
        box_up.start()

    @pl.when(d > 0)
    def _():
        box_down.start()

    to_up.wait_recv()
    to_down.wait_recv()
    for r in range(2):
        rows = pl.ds(r * SLOTS, SLOTS)
        xrim[rows, 0:RIM] = lax.dot_general(sel, halo_l[r], NT, preferred_element_type=F32).astype(BF16)
        xrim[rows, RIM : 2 * RIM] = lax.dot_general(sel, halo_r[r], NT, preferred_element_type=F32).astype(BF16)
    low = low_lanes(PAR)

    def plane_copy(k):
        return copy_to(send.at[k], prec.at[0, q], pl_s.at[k], pl_d.at[q], box=h * 32 + 2 * k + c)

    def cross_copy(k):
        return copy_to(send.at[k], prec.at[2, q], cr_s.at[k], cr_d.at[q], box=far_half + 2 * k + c)

    row, turn = q // 4, q % 4

    def shift(step, carry):
        t = (row + step) % 4
        parts = []
        for half in range(2):
            cols = pl.ds(pl.multiple_of(half * 1024 + 256 * t, 256), 256)
            rim_w = jnp.concatenate([w[0:RIM, cols], w[RIM + KCG :, cols]], axis=0)
            y = ybuf[:, cols] + jnp.dot(xrim[...], rim_w, preferred_element_type=F32)
            cc = cosine[:, cols]
            ss = sine[:, cols]
            re = im = None
            for o in range(8):
                yr = y[o * PAR : (o + 1) * PAR]
                yi = y[SLOTS + o * PAR : SLOTS + (o + 1) * PAR]
                co, so = cc[o : o + 1], ss[o : o + 1]
                tr = yr * co - yi * so
                ti = yr * so + yi * co
                re = tr if re is None else re + tr
                im = ti if im is None else im + ti
            parts.append((re, im))
        for u in range(2):
            for r in range(2):
                a = parts[0][r][:, 128 * u : 128 * u + 128]
                b = parts[1][r][:, 128 * u : 128 * u + 128]
                at = 128 * r
                send[4 * t + 2 * u, :, at : at + 128] = jnp.where(low, a, pltpu.roll(b, 64, 1)).astype(BF16)
                send[4 * t + 2 * u + 1, :, at : at + 128] = jnp.where(low, pltpu.roll(a, 64, 1), b).astype(BF16)
        for e in range(4):
            k = 4 * t + (turn + e) % 4
            cross_copy(k).start()

            @pl.when(q != k)
            def _():
                plane_copy(k).start()

        return carry

    lax.fori_loop(0, 4, shift, 0)

    prec[0, q] = send[q]

    def from_plane(k):
        return copy_to(send.at[k], prec.at[0, k], pl_s.at[k], pl_d.at[k], box=mate)

    def from_cross(k):
        return copy_to(send.at[k], prec.at[2, k], cr_s.at[k], cr_d.at[k], box=mate)

    def mate_copy(j, e):
        return copy_to(
            prec.at[j, pl.ds(4 * e, 4)], prec.at[j + 1, pl.ds(4 * e, 4)],
            co_s.at[2 * j + e], co_d.at[2 * j + e], box=mate,
        )

    def arrival(step):
        return (row + 4 - step) % 4

    for step in range(4):
        for e in range(4):
            k = 4 * arrival(step) + e

            @pl.when(q != k)
            def _():
                from_plane(k).wait_recv()

        mate_copy(0, arrival(step)).start()

    for i in range(6, 13):
        loads[i].wait()
    slots = lax.broadcasted_iota(jnp.int32, (8, 128), 0)
    for i in range(16):
        cols = pl.ds(128 * i, 128)
        s = psrc[:, cols]
        slot = ((lax.shift_right_logical(s, 10) ^ h) * 2) | ((lax.shift_right_logical(s, 5) & 1) ^ c)
        at = slot * 512 + (lax.shift_right_logical(s, 6) & 15) * 32 + (s & 31)
        sall[128 * i : 128 * i + 128] = at.astype(F32).T
        o = jnp.where(slots < pcnt[:, cols], poff[:, cols], OFFPAD)
        oall[128 * i : 128 * i + 128] = o.astype(F32).T
    for k in range(16):
        rows = pl.ds(pl.multiple_of(h * 1024 + 64 * k + 32 * c, 32), 32)
        smine[32 * k : 32 * k + 32] = sall[rows]
        omine[32 * k : 32 * k + 32] = oall[rows]

    wide = lax.broadcasted_iota(jnp.int32, (128, 1024), 1).astype(F32)

    def cross_hot(b, carry):
        rows = pl.ds(pl.multiple_of(128 * b, 128), 128)
        for m in range(8):
            ohx[pl.ds(pl.multiple_of(1024 * b, 1024) + 128 * m, 128)] = (
                (smine[rows, m : m + 1] - 1024.0 == wide).astype(F32).astype(BF16)
            )
        return carry

    lax.fori_loop(0, 4, cross_hot, 0)

    ctab[NOFF - 12 :] = jnp.zeros((OFFPAD - NOFF + 12, 2 * KCG), BF16)
    for n in range(4):
        cflat[...] = craw[:, :, 128 * n : 128 * n + 128].astype(F32).reshape(2 * NOFF, 128)
        for r in range(2):
            at = KCG * r + 128 * n
            ctab[0:NOFF, at : at + 128] = cflat[pl.ds(r, NOFF, stride=2), :].astype(BF16)

    rel = csrc[...] - d * 128
    pos = jnp.where(rel < 0, rel + 160, jnp.where(rel < 128, rel, rel + 32)).astype(F32)
    off = jnp.where(slots < ccnt[...], coff[...], OFFPAD).astype(F32)

    @pl.when(d > 0)
    def _():
        copy_to(bsend.at[0], box_b, box_s.at[0], box_d.at[0], box=mate).wait_recv()

    @pl.when(d < 63)
    def _():
        copy_to(bsend.at[1], box_a, box_s.at[1], box_d.at[1], box=mate).wait_recv()

    near_lists(own, box_b, box_a, ctab, pos.T, off.T, near, ohs, oht)

    t_far.wait_recv()
    t_second = copy_to(tparts.at[1], tparts.at[2], t_s.at[2], t_d.at[2], box=mate)
    t_second.start()
    t_mate.wait_recv()
    t_second.wait_recv()
    for j in range(4):
        hs = h + (j // 2) - 2 * h * (j // 2)
        cs = c + (j % 2) - 2 * c * (j % 2)
        at = pl.multiple_of(64 * hs + 32 * cs, 32)
        for r in range(2):
            tt[r, pl.ds(at, 32), :] = (tsend[r] if j == 0 else tparts[j - 1, r]).astype(F32)
    for r in range(2):
        tmat[:, 128 * r : 128 * r + 128] = tt[r].T.astype(BF16)

    narrow = lax.broadcasted_iota(jnp.int32, (128, OFFPAD), 1).astype(F32)
    for e in range(4):
        mate_copy(0, e).wait_recv()

    def own_half(b, carry):
        rows = pl.ds(pl.multiple_of(128 * b, 128), 128)
        block = pl.ds(pl.multiple_of(1024 * b, 1024), 1024)
        for m in range(8):
            oho[128 * m : 128 * m + 128] = (smine[rows, m : m + 1] == wide).astype(F32).astype(BF16)
            ohp[128 * m : 128 * m + 128] = (omine[rows, m : m + 1] == narrow).astype(F32).astype(BF16)
        gown[block] = jnp.dot(oho[...], prec[0:2].reshape(1024, 256), preferred_element_type=F32)
        tgat[block] = jnp.dot(ohp[...], tmat[...], preferred_element_type=F32)
        return carry

    lax.fori_loop(0, 4, own_half, 0)

    def gather_more(j, group):
        cols = pl.ds(pl.multiple_of(512 * (j - 2) + 128 * group, 128), 128)
        return lambda block: jnp.dot(
            ohx[block, cols], prec[j, pl.ds(4 * group, 4)].reshape(128, 256), preferred_element_type=F32
        )

    def accumulate(j, group):
        more = gather_more(j, group)

        def add(b, carry):
            block = pl.ds(pl.multiple_of(1024 * b, 1024), 1024)
            gown[block] = gown[block] + more(block)
            return carry

        lax.fori_loop(0, 4, add, 0)

    for step in range(4):
        for e in range(4):
            from_cross(4 * arrival(step) + e).wait_recv()
        mate_copy(2, arrival(step)).start()
        accumulate(2, arrival(step))
        if step:
            mate_copy(2, arrival(step - 1)).wait_recv()
            accumulate(3, arrival(step - 1))
    mate_copy(2, arrival(3)).wait_recv()

    def return_copy(k):
        return copy_to(fsend.at[k], frecv.at[q], re_s.at[k], re_d.at[q], box=h * 32 + 2 * k + c)

    def targets(step, carry):
        b = (row + step) % 4
        block = pl.ds(pl.multiple_of(1024 * b, 1024), 1024)
        p = gown[block] + gather_more(3, arrival(3))(block)
        tc = tgat[block]
        re = im = None
        for m in range(8):
            rows = slice(128 * m, 128 * m + 128)
            pr, pi = p[rows, 0:128], p[rows, 128:256]
            tr, ti = tc[rows, 0:128], tc[rows, 128:256]
            x = tr * pr - ti * pi
            y = tr * pi + ti * pr
            re = x if re is None else re + x
            im = y if im is None else im + y
        for e in range(4):
            fsend[4 * b + e, :, 0:128] = re[32 * e : 32 * e + 32].astype(BF16)
            fsend[4 * b + e, :, 128:256] = im[32 * e : 32 * e + 32].astype(BF16)
        for e in range(4):
            k = 4 * b + (turn + e) % 4

            @pl.when(q != k)
            def _():
                return_copy(k).start()

        return carry

    lax.fori_loop(0, 4, targets, 0)
    frecv[q] = fsend[q]

    for t in range(8):
        for k in range(2 * t, 2 * t + 2):

            @pl.when(q != k)
            def _():
                copy_to(fsend.at[k], frecv.at[k], re_s.at[k], re_d.at[k], box=mate).wait_recv()

        tiles = []
        for r in range(2):
            a = frecv[2 * t, :, 128 * r : 128 * r + 128].astype(F32)
            b = frecv[2 * t + 1, :, 128 * r : 128 * r + 128].astype(F32)
            tiles.append((jnp.where(low, a, pltpu.roll(b, 64, 1)), jnp.where(low, pltpu.roll(a, 64, 1), b)))
        for half in range(2):
            fr, fi = tiles[0][half], tiles[1][half]
            at = half * 1024 + 128 * t
            for o in range(8):
                co = cosine[o : o + 1, at : at + 128]
                so = sine[o : o + 1, at : at + 128]
                lslot[0, o * PAR : (o + 1) * PAR, at : at + 128] = (fr * co + fi * so).astype(BF16)
                lslot[1, o * PAR : (o + 1) * PAR, at : at + 128] = (fi * co - fr * so).astype(BF16)
    for r in range(2):
        lsel[r * 128 : (r + 1) * 128] = lax.dot_general(
            sel, lslot[r], (((0,), (0,)), ((), ())), preferred_element_type=F32
        ).astype(BF16)

    lows = lax.dot_general(w[0:RIM], lsel[...], NT, preferred_element_type=F32)
    highs = lax.dot_general(w[RIM + KCG :], lsel[...], NT, preferred_element_type=F32)
    for r in range(2):
        rsend[0, r] = lows[:, r * 128 : (r + 1) * 128].astype(BF16)
        rsend[1, r] = highs[:, r * 128 : (r + 1) * 128].astype(BF16)
    rim_down = copy_to(rsend.at[0], rim_hi, rim_s.at[0], rim_d.at[0], samp=gdown)
    rim_up = copy_to(rsend.at[1], rim_lo, rim_s.at[1], rim_d.at[1], samp=gup)

    @pl.when(g != 0)
    def _():
        rim_down.start()

    rim_up.start()

    @pl.when(g == 0)
    def _():
        rim_down.start()

    mids = lax.dot_general(w[RIM : RIM + KCG], lsel[...], NT, preferred_element_type=F32)
    for r in range(2):
        mid = mids[:, r * 128 : (r + 1) * 128].astype(BF16).astype(F32)
        out[r, RIM : KCG - RIM] = (near[r, RIM : KCG - RIM] + mid[RIM : KCG - RIM]).astype(BF16)
        near[r, 0:RIM] = near[r, 0:RIM] + mid[0:RIM]
        near[r, KCG - RIM :] = near[r, KCG - RIM :] + mid[KCG - RIM :]
    rim_down.wait_recv()
    rim_up.wait_recv()
    for r in range(2):
        out[r, 0:RIM] = (near[r, 0:RIM] + rim_lo[r].astype(F32)).astype(BF16)
        out[r, KCG - RIM :] = (near[r, KCG - RIM :] + rim_hi[r].astype(F32)).astype(BF16)

    to_up.wait_send()
    to_down.wait_send()
    t_far.wait_send()
    t_mate.wait_send()
    t_second.wait_send()

    @pl.when(d < 63)
    def _():
        box_up.wait_send()

    @pl.when(d > 0)
    def _():
        box_down.wait_send()

    for k in range(16):
        cross_copy(k).wait_send()

        @pl.when(q != k)
        def _():
            plane_copy(k).wait_send()
            return_copy(k).wait_send()

    for e in range(4):
        mate_copy(0, e).wait_send()
        mate_copy(2, e).wait_send()
    rim_down.wait_send()
    rim_up.wait_send()


def local(
    child_pattern,
    child_parent,
    child_octant,
    child_sources,
    child_offsets,
    child_counts,
    parent_sources,
    parent_offsets,
    parent_counts,
    interp_weights,
    shift_phase,
    child_table,
    parent_table,
):
    dma = pltpu.SemaphoreType.DMA
    vm = pl.BlockSpec(memory_space=pltpu.VMEM)
    anywhere = pl.BlockSpec(memory_space=pl.ANY)
    out = pl.pallas_call(
        whole,
        out_shape=pltpu.VMEM((2, KCG, 128), BF16),
        in_specs=[anywhere] * 13,
        out_specs=vm,
        scratch_shapes=[
            pltpu.VMEM((1, 128), jnp.int32),
            pltpu.VMEM((1, 128), jnp.int32),
            pltpu.VMEM((8, 128), jnp.int32),
            pltpu.VMEM((8, 128), jnp.int32),
            pltpu.VMEM((1, 128), jnp.int32),
            pltpu.VMEM((8, 2048), jnp.int32),
            pltpu.VMEM((8, 2048), jnp.int32),
            pltpu.VMEM((1, 2048), jnp.int32),
            pltpu.VMEM((2, KCG, 128), BF16),
            pltpu.VMEM((KCG + 2 * RIM, KPG), BF16),
            pltpu.VMEM((8, 1, KPG), F32),
            pltpu.VMEM((2, PAR, NOFF), BF16),
            pltpu.VMEM((NOFF, 2, KCG), BF16),
            pltpu.VMEM((OFFPAD, 2 * KCG), BF16),
            pltpu.VMEM((2 * NOFF, 128), F32),
            pltpu.VMEM((8, KPG), F32),
            pltpu.VMEM((8, KPG), F32),
            pltpu.VMEM((2, RIM, 128), BF16),
            pltpu.VMEM((2, RIM, 128), BF16),
            pltpu.VMEM((2, PAR, KCG), BF16),
            pltpu.VMEM((2, PAR, KCG), BF16),
            pltpu.VMEM((2, 2, PAR, KCG), BF16),
            pltpu.VMEM((2, PAR, OFFPAD), BF16),
            pltpu.VMEM((3, 2, PAR, OFFPAD), BF16),
            pltpu.VMEM((2 * SLOTS, KCG), BF16),
            pltpu.VMEM((2 * SLOTS, 2 * RIM), BF16),
            pltpu.VMEM((2 * SLOTS, KPG), F32),
            pltpu.VMEM((16, PAR, 256), BF16),
            pltpu.VMEM((4, 16, PAR, 256), BF16),
            pltpu.VMEM((2048, 8), F32),
            pltpu.VMEM((2048, 8), F32),
            pltpu.VMEM((512, 8), F32),
            pltpu.VMEM((512, 8), F32),
            pltpu.VMEM((4096, 1024), BF16),
            pltpu.VMEM((1024, 1024), BF16),
            pltpu.VMEM((1024, OFFPAD), BF16),
            pltpu.VMEM((4096, 256), F32),
            pltpu.VMEM((4096, 256), F32),
            pltpu.VMEM((OFFPAD, 256), BF16),
            pltpu.VMEM((2, 128, OFFPAD), F32),
            pltpu.VMEM((16, PAR, 256), BF16),
            pltpu.VMEM((16, PAR, 256), BF16),
            pltpu.VMEM((2, SLOTS, KPG), BF16),
            pltpu.VMEM((256, KPG), BF16),
            pltpu.VMEM((2, 2, RIM, 128), BF16),
            pltpu.VMEM((2, RIM, 128), BF16),
            pltpu.VMEM((2, RIM, 128), BF16),
            pltpu.VMEM((2, KCG, 128), F32),
            pltpu.VMEM((1024, 256), BF16),
            pltpu.VMEM((1024, OFFPAD), BF16),
        ]
        + [dma((n,)) for n in (13, 2, 2, 2, 2, 3, 3, 16, 16, 16, 16, 8, 8, 16, 16, 2, 2)],
        compiler_params=pltpu.CompilerParams(
            collective_id=0, has_side_effects=True, vmem_limit_bytes=60000 * 1024
        ),
    )(
        child_pattern[:, 0],
        jnp.transpose(parent_table[:, :, 0, :], (0, 2, 1)),
        shift_phase,
        interp_weights,
        child_parent[None, :],
        child_octant[None, :],
        child_sources.T,
        child_offsets.T,
        child_counts[None, :],
        parent_sources.T,
        parent_offsets.T,
        parent_counts[None, :],
        jnp.transpose(child_table[:, :, 0, :], (1, 0, 2)),
    )
    return out[:, None]


def solution(mesh):
    return jax.shard_map(
        local,
        mesh=mesh,
        in_specs=(
            P(None, "samp", None, "box"),
            P("box"),
            P("box"),
            P("box", None),
            P("box", None),
            P("box"),
            P(),
            P(),
            P(),
            P(),
            P(None, "samp", None),
            P(None, None, "samp", None),
            P(None, None, "samp", "box"),
        ),
        out_specs=P(None, "samp", None, "box"),
        check_vma=False,
    )
```

```python
import functools

import jax
import jax.numpy as jnp
from jax import lax
from jax.experimental import pallas as pl
from jax.experimental.pallas import tpu as pltpu
from jax.sharding import PartitionSpec as P

PAR = 32
KCG = 512
KPG = 2048
RIM = 64
NOFF = 316
OFFPAD = 384
SLOTS = 256
F32 = jnp.float32
BF16 = jnp.bfloat16
NT = (((1,), (1,)), ((), ()))


def slot_matrix(slot_row):
    rows = lax.broadcasted_iota(jnp.int32, (SLOTS, 128), 0)
    return (rows == slot_row).astype(F32).astype(BF16)


def low_lanes(rows):
    return lax.broadcasted_iota(jnp.int32, (rows, 128), 1) < 64


def copy_to(src, dst, send_sem, recv_sem, **device):
    return pltpu.make_async_remote_copy(
        src_ref=src,
        dst_ref=dst,
        send_sem=send_sem,
        recv_sem=recv_sem,
        device_id=device,
        device_id_type=pl.DeviceIdType.MESH,
    )


def near_lists(own, before, after, table, post, offt, near, ohs, oht):
    srow = lax.broadcasted_iota(jnp.int32, (128, 256), 1).astype(F32)
    trow = lax.broadcasted_iota(jnp.int32, (128, OFFPAD), 1).astype(F32)
    for m in range(8):
        ohs[m * 128 : (m + 1) * 128] = (post[:, m : m + 1] == srow).astype(F32).astype(BF16)
        oht[m * 128 : (m + 1) * 128] = (offt[:, m : m + 1] == trow).astype(F32).astype(BF16)
    for n in range(2):
        at = 256 * n
        ts, ps = [], []
        for r in range(2):
            ts.append(jnp.dot(oht[...], table[:, r * 512 + at : r * 512 + at + 256], preferred_element_type=F32))
            halo = jnp.concatenate([before[r, :, at : at + 256], after[r, :, at : at + 256]], axis=0)
            p = lax.dot_general(ohs[:, 0:128], own[r, at : at + 256], NT, preferred_element_type=F32)
            ps.append(p + jnp.dot(ohs[:, 128:192], halo, preferred_element_type=F32))
        re = ts[0] * ps[0] - ts[1] * ps[1]
        im = ts[0] * ps[1] + ts[1] * ps[0]
        for r, v in enumerate((re, im)):
            total = v[0:128]
            for m in range(1, 8):
                total = total + v[m * 128 : (m + 1) * 128]
            near[r, at : at + 256] = total.T


def whole(
    own_h, tpar_h, phase_h, w_h, cpar_h, coct_h, csrc_h, coff_h, ccnt_h, psrc_h, poff_h, pcnt_h, ctab_h,
    out,
    cpar, coct, csrc, coff, ccnt, psrc, poff, pcnt,
    own, w, phase, tpar, craw, ctab, cflat, cosine, sine,
    halo_l, halo_r, box_b, box_a, bsend, tsend, tparts, xown, xrim, ybuf, send, prec,
    sall, oall, smine, omine, ohx, oho, ohp, gown, tgat, tmat, tt,
    fsend, frecv, lslot, lsel, rsend, rim_lo, rim_hi, near, ohs, oht,
    in_s, halo_s, halo_d, box_s, box_d, t_s, t_d, pl_s, pl_d, cr_s, cr_d, co_s, co_d, re_s, re_d, rim_s, rim_d, ready,
):
    d = lax.axis_index("box")
    g = lax.axis_index("samp")
    h, q, c = d // 32, (d // 2) % 16, d % 2
    gup, gdown = (g + 1) % 8, (g + 7) % 8
    mate = d + 1 - 2 * c
    far_half = (1 - h) * 32

    barrier = pltpu.get_barrier_semaphore()

    def greet(**device):
        pl.semaphore_signal(barrier, inc=1, device_id=device, device_id_type=pl.DeviceIdType.MESH)

    @pl.when(h == 0)
    def _():
        for k in range(16):
            greet(box=32 + 2 * k + c)

    greet(samp=gup)
    greet(samp=gdown)
    for k in range(16):

        @pl.when(q != k)
        def _():
            greet(box=h * 32 + 2 * k + c)

    greet(box=mate)

    @pl.when(d < 63)
    def _():
        greet(box=d + 1)

    @pl.when(d > 0)
    def _():
        greet(box=d - 1)

    pairs = (
        (own_h, own), (tpar_h, tpar), (cpar_h, cpar), (coct_h, coct), (phase_h, phase), (w_h, w), (psrc_h, psrc), (poff_h, poff),
        (pcnt_h, pcnt), (csrc_h, csrc), (coff_h, coff), (ccnt_h, ccnt), (ctab_h, craw),
    )
    loads = [pltpu.make_async_copy(a, b, in_s.at[i]) for i, (a, b) in enumerate(pairs)]
    for load in loads:
        load.start()

    @pl.when(d == 0)
    def _():
        box_b[...] = jnp.zeros_like(box_b)

    @pl.when(d == 63)
    def _():
        box_a[...] = jnp.zeros_like(box_a)

    loads[0].wait()
    pl.semaphore_wait(barrier, 18 + 16 * h + (d < 63).astype(jnp.int32) + (d > 0).astype(jnp.int32))

    to_up = copy_to(own.at[:, KCG - RIM :], halo_l, halo_s.at[0], halo_d.at[0], samp=gup)
    to_down = copy_to(own.at[:, :RIM], halo_r, halo_s.at[1], halo_d.at[1], samp=gdown)

    @pl.when(h == 1)
    def _():
        for k in range(16):
            pl.semaphore_signal(
                ready, inc=1, device_id={"box": 2 * k + c}, device_id_type=pl.DeviceIdType.MESH
            )

    to_up.start()
    to_down.start()
    loads[1].wait()
    tsend[...] = jnp.zeros_like(tsend)
    tsend[:, :, 0:NOFF] = tpar[...]
    t_far = copy_to(tsend, tparts.at[1], t_s.at[0], t_d.at[0], box=far_half + 2 * q + c)
    t_mate = copy_to(tsend, tparts.at[0], t_s.at[1], t_d.at[1], box=mate)
    t_mate.start()

    @pl.when(h == 1)
    def _():
        t_far.start()

    pick = lax.broadcasted_iota(jnp.int32, (PAR, 128), 0)
    lane = lax.broadcasted_iota(jnp.int32, (PAR, 128), 1)
    last = (pick + 96 == lane).astype(F32).astype(BF16)
    first = (pick == lane).astype(F32).astype(BF16)
    for r in range(2):
        bsend[0, r] = lax.dot_general(last, own[r], NT, preferred_element_type=F32).astype(BF16)
        bsend[1, r] = lax.dot_general(first, own[r], NT, preferred_element_type=F32).astype(BF16)
    box_up = copy_to(bsend.at[0], box_b, box_s.at[0], box_d.at[0], box=d + 1)
    box_down = copy_to(bsend.at[1], box_a, box_s.at[1], box_d.at[1], box=d - 1)

    @pl.when(d < 63)
    def _():
        box_up.start()

    @pl.when(d > 0)
    def _():
        box_down.start()

    for i in range(2, 6):
        loads[i].wait()
    sel = slot_matrix(coct[...] * PAR + cpar[...] - d * PAR)
    for r in range(2):
        xown[r * SLOTS : (r + 1) * SLOTS] = lax.dot_general(
            sel, own[r], NT, preferred_element_type=F32
        ).astype(BF16)
    for o in range(8):
        cosine[o : o + 1] = phase[o]
    angles = cosine[...]
    cosine[...] = jnp.cos(angles)
    sine[...] = jnp.sin(angles)
    for t in range(8):
        ybuf[:, 256 * t : 256 * t + 256] = jnp.dot(
            xown[...], w[RIM : RIM + KCG, 256 * t : 256 * t + 256], preferred_element_type=F32
        )

    to_up.wait_recv()
    to_down.wait_recv()
    for r in range(2):
        rows = pl.ds(r * SLOTS, SLOTS)
        xrim[rows, 0:RIM] = lax.dot_general(sel, halo_l[r], NT, preferred_element_type=F32).astype(BF16)
        xrim[rows, RIM : 2 * RIM] = lax.dot_general(sel, halo_r[r], NT, preferred_element_type=F32).astype(BF16)
    low = low_lanes(PAR)

    def plane_copy(k):
        return copy_to(send.at[k], prec.at[0, q], pl_s.at[k], pl_d.at[q], box=h * 32 + 2 * k + c)

    def cross_copy(k):
        return copy_to(send.at[k], prec.at[2, q], cr_s.at[k], cr_d.at[q], box=far_half + 2 * k + c)

    row, turn = q // 4, q % 4

    def shift(step, carry):
        t = (row + step) % 4
        parts = []
        for half in range(2):
            cols = pl.ds(pl.multiple_of(half * 1024 + 256 * t, 256), 256)
            rim_w = jnp.concatenate([w[0:RIM, cols], w[RIM + KCG :, cols]], axis=0)
            y = ybuf[:, cols] + jnp.dot(xrim[...], rim_w, preferred_element_type=F32)
            cc = cosine[:, cols]
            ss = sine[:, cols]
            re = im = None
            for o in range(8):
                yr = y[o * PAR : (o + 1) * PAR]
                yi = y[SLOTS + o * PAR : SLOTS + (o + 1) * PAR]
                co, so = cc[o : o + 1], ss[o : o + 1]
                tr = yr * co - yi * so
                ti = yr * so + yi * co
                re = tr if re is None else re + tr
                im = ti if im is None else im + ti
            parts.append((re, im))
        for u in range(2):
            for r in range(2):
                a = parts[0][r][:, 128 * u : 128 * u + 128]
                b = parts[1][r][:, 128 * u : 128 * u + 128]
                at = 128 * r
                send[4 * t + 2 * u, :, at : at + 128] = jnp.where(low, a, pltpu.roll(b, 64, 1)).astype(BF16)
                send[4 * t + 2 * u + 1, :, at : at + 128] = jnp.where(low, pltpu.roll(a, 64, 1), b).astype(BF16)
        for e in range(4):
            k = 4 * t + (turn + e) % 4

            @pl.when(h == 1)
            def _():
                cross_copy(k).start()

            @pl.when(q != k)
            def _():
                plane_copy(k).start()

        return carry

    lax.fori_loop(0, 4, shift, 0)

    @pl.when(h == 0)
    def _():
        pl.semaphore_wait(ready, 16)
        t_far.start()
        for step in range(4):
            for e in range(4):
                cross_copy(4 * ((row + step) % 4) + (turn + e) % 4).start()


    prec[0, q] = send[q]

    def from_plane(k):
        return copy_to(send.at[k], prec.at[0, k], pl_s.at[k], pl_d.at[k], box=mate)

    def from_cross(k):
        return copy_to(send.at[k], prec.at[2, k], cr_s.at[k], cr_d.at[k], box=mate)

    def mate_copy(j, e):
        return copy_to(
            prec.at[j, pl.ds(4 * e, 4)], prec.at[j + 1, pl.ds(4 * e, 4)],
            co_s.at[2 * j + e], co_d.at[2 * j + e], box=mate,
        )

    def arrival(step):
        return (row + 4 - step) % 4

    for step in range(4):
        for e in range(4):
            k = 4 * arrival(step) + e

            @pl.when(q != k)
            def _():
                from_plane(k).wait_recv()

        mate_copy(0, arrival(step)).start()

    for i in range(6, 13):
        loads[i].wait()
    slots = lax.broadcasted_iota(jnp.int32, (8, 128), 0)
    for i in range(16):
        cols = pl.ds(128 * i, 128)
        s = psrc[:, cols]
        slot = ((lax.shift_right_logical(s, 10) ^ h) * 2) | ((lax.shift_right_logical(s, 5) & 1) ^ c)
        at = slot * 512 + (lax.shift_right_logical(s, 6) & 15) * 32 + (s & 31)
        sall[128 * i : 128 * i + 128] = at.astype(F32).T
        o = jnp.where(slots < pcnt[:, cols], poff[:, cols], OFFPAD)
        oall[128 * i : 128 * i + 128] = o.astype(F32).T
    for k in range(16):
        rows = pl.ds(pl.multiple_of(h * 1024 + 64 * k + 32 * c, 32), 32)
        smine[32 * k : 32 * k + 32] = sall[rows]
        omine[32 * k : 32 * k + 32] = oall[rows]

    wide = lax.broadcasted_iota(jnp.int32, (128, 1024), 1).astype(F32)

    def cross_hot(b, carry):
        rows = pl.ds(pl.multiple_of(128 * b, 128), 128)
        for m in range(8):
            ohx[pl.ds(pl.multiple_of(1024 * b, 1024) + 128 * m, 128)] = (
                (smine[rows, m : m + 1] - 1024.0 == wide).astype(F32).astype(BF16)
            )
        return carry

    lax.fori_loop(0, 4, cross_hot, 0)

    ctab[NOFF - 12 :] = jnp.zeros((OFFPAD - NOFF + 12, 2 * KCG), BF16)
    for n in range(4):
        cflat[...] = craw[:, :, 128 * n : 128 * n + 128].astype(F32).reshape(2 * NOFF, 128)
        for r in range(2):
            at = KCG * r + 128 * n
            ctab[0:NOFF, at : at + 128] = cflat[pl.ds(r, NOFF, stride=2), :].astype(BF16)

    rel = csrc[...] - d * 128
    pos = jnp.where(rel < 0, rel + 160, jnp.where(rel < 128, rel, rel + 32)).astype(F32)
    off = jnp.where(slots < ccnt[...], coff[...], OFFPAD).astype(F32)

    @pl.when(d > 0)
    def _():
        copy_to(bsend.at[0], box_b, box_s.at[0], box_d.at[0], box=mate).wait_recv()

    @pl.when(d < 63)
    def _():
        copy_to(bsend.at[1], box_a, box_s.at[1], box_d.at[1], box=mate).wait_recv()

    near_lists(own, box_b, box_a, ctab, pos.T, off.T, near, ohs, oht)

    t_far.wait_recv()
    t_second = copy_to(tparts.at[1], tparts.at[2], t_s.at[2], t_d.at[2], box=mate)
    t_second.start()
    t_mate.wait_recv()
    t_second.wait_recv()
    for j in range(4):
        hs = h + (j // 2) - 2 * h * (j // 2)
        cs = c + (j % 2) - 2 * c * (j % 2)
        at = pl.multiple_of(64 * hs + 32 * cs, 32)
        for r in range(2):
            tt[r, pl.ds(at, 32), :] = (tsend[r] if j == 0 else tparts[j - 1, r]).astype(F32)
    for r in range(2):
        tmat[:, 128 * r : 128 * r + 128] = tt[r].T.astype(BF16)

    narrow = lax.broadcasted_iota(jnp.int32, (128, OFFPAD), 1).astype(F32)
    for e in range(4):
        mate_copy(0, e).wait_recv()

    def own_half(b, carry):
        rows = pl.ds(pl.multiple_of(128 * b, 128), 128)
        block = pl.ds(pl.multiple_of(1024 * b, 1024), 1024)
        for m in range(8):
            oho[128 * m : 128 * m + 128] = (smine[rows, m : m + 1] == wide).astype(F32).astype(BF16)
            ohp[128 * m : 128 * m + 128] = (omine[rows, m : m + 1] == narrow).astype(F32).astype(BF16)
        gown[block] = jnp.dot(oho[...], prec[0:2].reshape(1024, 256), preferred_element_type=F32)
        tgat[block] = jnp.dot(ohp[...], tmat[...], preferred_element_type=F32)
        return carry

    lax.fori_loop(0, 4, own_half, 0)

    for step in range(4):
        for e in range(4):
            from_cross(4 * arrival(step) + e).wait_recv()
        mate_copy(2, arrival(step)).start()
    for e in range(4):
        mate_copy(2, e).wait_recv()

    def return_copy(k):
        return copy_to(fsend.at[k], frecv.at[q], re_s.at[k], re_d.at[q], box=h * 32 + 2 * k + c)

    def targets(step, carry):
        b = (row + step) % 4
        block = pl.ds(pl.multiple_of(1024 * b, 1024), 1024)
        p = gown[block] + jnp.dot(ohx[block], prec[2:4].reshape(1024, 256), preferred_element_type=F32)
        tc = tgat[block]
        re = im = None
        for m in range(8):
            rows = slice(128 * m, 128 * m + 128)
            pr, pi = p[rows, 0:128], p[rows, 128:256]
            tr, ti = tc[rows, 0:128], tc[rows, 128:256]
            x = tr * pr - ti * pi
            y = tr * pi + ti * pr
            re = x if re is None else re + x
            im = y if im is None else im + y
        for e in range(4):
            fsend[4 * b + e, :, 0:128] = re[32 * e : 32 * e + 32].astype(BF16)
            fsend[4 * b + e, :, 128:256] = im[32 * e : 32 * e + 32].astype(BF16)
        for e in range(4):
            k = 4 * b + (turn + e) % 4

            @pl.when(q != k)
            def _():
                return_copy(k).start()

        return carry

    lax.fori_loop(0, 4, targets, 0)
    frecv[q] = fsend[q]

    for t in range(8):
        for k in range(2 * t, 2 * t + 2):

            @pl.when(q != k)
            def _():
                copy_to(fsend.at[k], frecv.at[k], re_s.at[k], re_d.at[k], box=mate).wait_recv()

        tiles = []
        for r in range(2):
            a = frecv[2 * t, :, 128 * r : 128 * r + 128].astype(F32)
            b = frecv[2 * t + 1, :, 128 * r : 128 * r + 128].astype(F32)
            tiles.append((jnp.where(low, a, pltpu.roll(b, 64, 1)), jnp.where(low, pltpu.roll(a, 64, 1), b)))
        for half in range(2):
            fr, fi = tiles[0][half], tiles[1][half]
            at = half * 1024 + 128 * t
            for o in range(8):
                co = cosine[o : o + 1, at : at + 128]
                so = sine[o : o + 1, at : at + 128]
                lslot[0, o * PAR : (o + 1) * PAR, at : at + 128] = (fr * co + fi * so).astype(BF16)
                lslot[1, o * PAR : (o + 1) * PAR, at : at + 128] = (fi * co - fr * so).astype(BF16)
    for r in range(2):
        lsel[r * 128 : (r + 1) * 128] = lax.dot_general(
            sel, lslot[r], (((0,), (0,)), ((), ())), preferred_element_type=F32
        ).astype(BF16)

    lows = lax.dot_general(w[0:RIM], lsel[...], NT, preferred_element_type=F32)
    highs = lax.dot_general(w[RIM + KCG :], lsel[...], NT, preferred_element_type=F32)
    for r in range(2):
        rsend[0, r] = lows[:, r * 128 : (r + 1) * 128].astype(BF16)
        rsend[1, r] = highs[:, r * 128 : (r + 1) * 128].astype(BF16)
    rim_down = copy_to(rsend.at[0], rim_hi, rim_s.at[0], rim_d.at[0], samp=gdown)
    rim_up = copy_to(rsend.at[1], rim_lo, rim_s.at[1], rim_d.at[1], samp=gup)
    rim_down.start()
    rim_up.start()
    mids = lax.dot_general(w[RIM : RIM + KCG], lsel[...], NT, preferred_element_type=F32)
    for r in range(2):
        mid = mids[:, r * 128 : (r + 1) * 128].astype(BF16).astype(F32)
        out[r, RIM : KCG - RIM] = (near[r, RIM : KCG - RIM] + mid[RIM : KCG - RIM]).astype(BF16)
        near[r, 0:RIM] = near[r, 0:RIM] + mid[0:RIM]
        near[r, KCG - RIM :] = near[r, KCG - RIM :] + mid[KCG - RIM :]
    rim_down.wait_recv()
    rim_up.wait_recv()
    for r in range(2):
        out[r, 0:RIM] = (near[r, 0:RIM] + rim_lo[r].astype(F32)).astype(BF16)
        out[r, KCG - RIM :] = (near[r, KCG - RIM :] + rim_hi[r].astype(F32)).astype(BF16)

    to_up.wait_send()
    to_down.wait_send()
    t_far.wait_send()
    t_mate.wait_send()
    t_second.wait_send()

    @pl.when(d < 63)
    def _():
        box_up.wait_send()

    @pl.when(d > 0)
    def _():
        box_down.wait_send()

    for k in range(16):
        cross_copy(k).wait_send()

        @pl.when(q != k)
        def _():
            plane_copy(k).wait_send()
            return_copy(k).wait_send()

    for e in range(4):
        mate_copy(0, e).wait_send()
        mate_copy(2, e).wait_send()
    rim_down.wait_send()
    rim_up.wait_send()


def local(
    child_pattern,
    child_parent,
    child_octant,
    child_sources,
    child_offsets,
    child_counts,
    parent_sources,
    parent_offsets,
    parent_counts,
    interp_weights,
    shift_phase,
    child_table,
    parent_table,
):
    dma = pltpu.SemaphoreType.DMA
    vm = pl.BlockSpec(memory_space=pltpu.VMEM)
    anywhere = pl.BlockSpec(memory_space=pl.ANY)
    out = pl.pallas_call(
        whole,
        out_shape=pltpu.VMEM((2, KCG, 128), BF16),
        in_specs=[anywhere] * 13,
        out_specs=vm,
        scratch_shapes=[
            pltpu.VMEM((1, 128), jnp.int32),
            pltpu.VMEM((1, 128), jnp.int32),
            pltpu.VMEM((8, 128), jnp.int32),
            pltpu.VMEM((8, 128), jnp.int32),
            pltpu.VMEM((1, 128), jnp.int32),
            pltpu.VMEM((8, 2048), jnp.int32),
            pltpu.VMEM((8, 2048), jnp.int32),
            pltpu.VMEM((1, 2048), jnp.int32),
            pltpu.VMEM((2, KCG, 128), BF16),
            pltpu.VMEM((KCG + 2 * RIM, KPG), BF16),
            pltpu.VMEM((8, 1, KPG), F32),
            pltpu.VMEM((2, PAR, NOFF), BF16),
            pltpu.VMEM((NOFF, 2, KCG), BF16),
            pltpu.VMEM((OFFPAD, 2 * KCG), BF16),
            pltpu.VMEM((2 * NOFF, 128), F32),
            pltpu.VMEM((8, KPG), F32),
            pltpu.VMEM((8, KPG), F32),
            pltpu.VMEM((2, RIM, 128), BF16),
            pltpu.VMEM((2, RIM, 128), BF16),
            pltpu.VMEM((2, PAR, KCG), BF16),
            pltpu.VMEM((2, PAR, KCG), BF16),
            pltpu.VMEM((2, 2, PAR, KCG), BF16),
            pltpu.VMEM((2, PAR, OFFPAD), BF16),
            pltpu.VMEM((3, 2, PAR, OFFPAD), BF16),
            pltpu.VMEM((2 * SLOTS, KCG), BF16),
            pltpu.VMEM((2 * SLOTS, 2 * RIM), BF16),
            pltpu.VMEM((2 * SLOTS, KPG), F32),
            pltpu.VMEM((16, PAR, 256), BF16),
            pltpu.VMEM((4, 16, PAR, 256), BF16),
            pltpu.VMEM((2048, 8), F32),
            pltpu.VMEM((2048, 8), F32),
            pltpu.VMEM((512, 8), F32),
            pltpu.VMEM((512, 8), F32),
            pltpu.VMEM((4096, 1024), BF16),
            pltpu.VMEM((1024, 1024), BF16),
            pltpu.VMEM((1024, OFFPAD), BF16),
            pltpu.VMEM((4096, 256), F32),
            pltpu.VMEM((4096, 256), F32),
            pltpu.VMEM((OFFPAD, 256), BF16),
            pltpu.VMEM((2, 128, OFFPAD), F32),
            pltpu.VMEM((16, PAR, 256), BF16),
            pltpu.VMEM((16, PAR, 256), BF16),
            pltpu.VMEM((2, SLOTS, KPG), BF16),
            pltpu.VMEM((256, KPG), BF16),
            pltpu.VMEM((2, 2, RIM, 128), BF16),
            pltpu.VMEM((2, RIM, 128), BF16),
            pltpu.VMEM((2, RIM, 128), BF16),
            pltpu.VMEM((2, KCG, 128), F32),
            pltpu.VMEM((1024, 256), BF16),
            pltpu.VMEM((1024, OFFPAD), BF16),
        ]
        + [dma((n,)) for n in (13, 2, 2, 2, 2, 3, 3, 16, 16, 16, 16, 8, 8, 16, 16, 2, 2)]
        + [pltpu.SemaphoreType.REGULAR],
        compiler_params=pltpu.CompilerParams(
            collective_id=0, has_side_effects=True, vmem_limit_bytes=60000 * 1024
        ),
    )(
        child_pattern[:, 0],
        jnp.transpose(parent_table[:, :, 0, :], (0, 2, 1)),
        shift_phase,
        interp_weights,
        child_parent[None, :],
        child_octant[None, :],
        child_sources.T,
        child_offsets.T,
        child_counts[None, :],
        parent_sources.T,
        parent_offsets.T,
        parent_counts[None, :],
        jnp.transpose(child_table[:, :, 0, :], (1, 0, 2)),
    )
    return out[:, None]


def solution(mesh):
    return jax.shard_map(
        local,
        mesh=mesh,
        in_specs=(
            P(None, "samp", None, "box"),
            P("box"),
            P("box"),
            P("box", None),
            P("box", None),
            P("box"),
            P(),
            P(),
            P(),
            P(),
            P(None, "samp", None),
            P(None, None, "samp", None),
            P(None, None, "samp", "box"),
        ),
        out_specs=P(None, "samp", None, "box"),
        check_vma=False,
    )
```
